32 devices in a mesh: dp: 8 (over z, y), expert: 4 (over x, core).
Axes of the slice: x: 2, y: 2, z: 4, core: 2. Of those that a mesh axis runs over, the one named last changes fastest.
Arguments:
- tokens: bfloat16 [12288, 768], P(('dp', 'expert')), may hold values from -6 to 6
- groups: int32 [32, 384], P(('dp', 'expert')), may hold values from 0 to 1, never falling along the last dimension, each value on 1 to 261 neighbouring positions
- key_mask: int32 [12288], P(('dp', 'expert')), may hold values 0 or 1
- routes: int32 [12288, 1], P(('dp', 'expert')), may hold values from 0 to 2; in each aligned block of 384 rows (0 to 383, 384 to 767, ...) at most 144 rows name the same one
- query_weight: bfloat16 [2, 768, 768], P(None, ('dp', 'expert')), may hold values from -0.21875 to 0.21875
- key_weight: bfloat16 [2, 768, 768], P(None, ('dp', 'expert')), may hold values from -0.21875 to 0.21875
- value_weight: bfloat16 [2, 768, 768], P(None, ('dp', 'expert')), may hold values from -0.21875 to 0.21875
- output_weight: bfloat16 [2, 768, 768], P(None, ('dp', 'expert')), may hold values from -1.75 to 1.75
- norm_first: bfloat16 [2, 768], P(None, ('dp', 'expert')), may hold values from 0.25 to 1.75
- norm_second: bfloat16 [2, 768], P(None, ('dp', 'expert')), may hold values from 0.25 to 1.75
- expert_in: bfloat16 [2, 3, 768, 3072], P(None, None, 'dp', 'expert'), may hold values from -0.21875 to 0.21875
- expert_out: bfloat16 [2, 3, 3072, 768], P(None, None, 'expert', 'dp'), may hold values from -0.109375 to 0.109375
- cotangent: float32 [12288, 768], P(('dp', 'expert')), may hold values from -6 to 6
Outputs:
- mixed: bfloat16 [12288, 768], P(('dp', 'expert'))
- delta_tokens: float32 [12288, 768], P(('dp', 'expert'))
- delta_query: float32 [2, 768, 768], P(None, ('dp', 'expert'))
- delta_key: float32 [2, 768, 768], P(None, ('dp', 'expert'))
- delta_value: float32 [2, 768, 768], P(None, ('dp', 'expert'))
- delta_output: float32 [2, 768, 768], P(None, ('dp', 'expert'))
- delta_first: float32 [2, 768], P(None, ('dp', 'expert'))
- delta_second: float32 [2, 768], P(None, ('dp', 'expert'))
- delta_in: float32 [2, 3, 768, 3072], P(None, None, 'dp', 'expert')
- delta_out: float32 [2, 3, 3072, 768], P(None, None, 'expert', 'dp')
The draws below stay inside these ranges and needn't reach their ends.
Inputs may be any that keep to these rules, and one draw needn't show every extreme that they name: Each device's block holds 2 groups numbered in order, each of 1 to 261 tokens. `routes`: among the 384 tokens of one device no expert is named more than 144 times; on some devices one expert is named exactly 144 times.
All inputs are finite; a program needn't handle non-finite values. No bound on the sum of `key_mask` on one device may be relied on, other than what follows from the above.
Results may differ from the reference program's by a relative error of at most 0.024.
Values may be sent and summed in bfloat16 or wider, within the bound.
No kernel may reach another device: no remote copies, remote signals or barrier semaphores. Data moves between devices by JAX's collectives and lax.ppermute only.
A program may use at most 256 MiB of HBM per device.

```python
import math
import jax
import jax.numpy as jnp
import numpy as np
from jax import lax

D = 768
HEADS = 12
HEAD_DIM = 64
FF = 3072
EXPERTS = 3
LAYERS = 2
GROUP_LEN = 261
TOK_DEV = 384
GROUPS_DEV = 2
MOST = 144
TOKENS = 12288
DEVICES_ALL = 32
N_DP = 8
N_EXPERT = 4


def plant(entries, key, low, high):
    longest = entries.shape.index(max(entries.shape))
    spots = []
    for shift in (0, 1):
        where = [jax.random.randint(jax.random.fold_in(key, axis), (), 0, length) for axis, length in enumerate(entries.shape)]
        where[longest] = (where[longest] + shift) % entries.shape[longest]
        spots.append(tuple(where))
    return entries.at[spots[0]].set(low).at[spots[1]].set(high)


def steps_of(stream_key, shape, split, smallest, largest):
    level, own = 1.0, jax.random.fold_in(stream_key, 6)
    for dim, blocks in split:
        draws = jnp.exp(jax.random.uniform(jax.random.fold_in(own, dim), (blocks,), jnp.float32, smallest / len(split), largest / len(split)))
        level = level * jnp.repeat(draws, shape[dim] // blocks).reshape([-1 if axis == dim else 1 for axis in range(len(shape))])
    return level


def split_up(count, total, most, skew):
    weights = [(1 << 20) // math.isqrt(rank ** skew) + 1 for rank in range(2, count + 1)]
    spare, holding = total - most - (count - 1), [1] * (count - 1)
    while spare > 0:
        free = [i for i in range(count - 1) if holding[i] < most]
        mass, remaining = sum([weights[i] for i in free]), spare
        for i in free:
            addition = min(most - holding[i], max(1, remaining * weights[i] // mass), spare)
            holding[i] = holding[i] + addition
            spare = spare - addition
    return np.array([most] + holding)


def uneven(rng, number_of, total, limit, skew):
    if number_of == 2:
        one = jax.random.randint(rng, (), max(1, total - limit), min(limit, total - 1) + 1)
        return jnp.stack([one, total - one])
    tallies = jnp.asarray(split_up(number_of, total, limit, skew), jnp.int32)
    twos = (number_of - 1) // 2
    source_of, taker = tallies[1:1 + 2 * twos:2], tallies[2:2 + 2 * twos:2]
    slack = jnp.minimum(source_of - 1, limit - taker)
    passed = jax.random.randint(jax.random.fold_in(rng, 1), (twos,), 0, 1 << 20) % (slack + 1)
    tallies = tallies.at[1:1 + 2 * twos:2].set(source_of - passed).at[2:2 + 2 * twos:2].set(taker + passed)
    return tallies[jax.random.permutation(jax.random.fold_in(rng, 2), number_of)]


def shared_out(stream_key, own, number, rows, count, top, bound, skew):
    order = jax.random.permutation(stream_key, count)
    packed, ordinary = portions_of(count, rows * top, bound, skew, True), portions_of(count, rows * top, bound, skew, False)
    places = jnp.arange(count)

    def named(sizes, rotation):
        used = int((sizes > 0).sum())
        fixed = max(1, used // 4)
        moved = fixed + (places - fixed + rotation * (used - fixed)) % max(1, count - fixed)
        return jnp.zeros((count,), jnp.int32).at[order[jnp.where(places < fixed, places, moved)]].set(jnp.asarray(sizes, jnp.int32))

    sizes = jnp.where(number % 4 == 0, named(packed, number // 4), named(ordinary, number - number // 4 - 1))
    mixed = jax.random.permutation(jax.random.fold_in(own, 3), count)
    donor, receiver = mixed[0:count // 2 * 2:2], mixed[1:count // 2 * 2:2]
    slack = jnp.minimum(sizes[donor] - 1, bound - sizes[receiver]) // 2
    slack = jnp.where((donor == order[0]) | (receiver == order[0]) | (sizes[receiver] == 0), 0, jnp.maximum(slack, 0))
    moved = jax.random.randint(jax.random.fold_in(own, 4), (count // 2,), 0, 1 << 20) % (slack + 1)
    sizes = sizes.at[donor].add(-moved).at[receiver].add(moved)
    labels = jnp.searchsorted(jnp.cumsum(sizes), jnp.arange(rows * top), side="right").astype(jnp.int32)
    listing = labels.reshape(top, rows).T
    listing = listing[jax.random.permutation(jax.random.fold_in(own, 1), rows)]
    rotation = jax.random.randint(jax.random.fold_in(own, 2), (rows, 1), 0, top)
    return jnp.take_along_axis(listing, (jnp.arange(top)[None, :] + rotation) % top, axis=1)


def portions_of(number_of, total, most, slope, full):
    portions = [(1 << 20) // math.isqrt(rank ** slope) + 1 for rank in range(1, number_of + 1)]
    largest = most if full else min(most, max(-(-total // number_of), total * portions[0] // sum(portions)))
    least = 1 if total - largest >= number_of - 1 else 0
    counts, spare = [largest] + [least] * (number_of - 1), total - largest - least * (number_of - 1)
    while spare > 0:
        movable = [i for i in range(1, number_of) if counts[i] < largest] or [i for i in range(1, number_of) if counts[i] < most]
        mass, left = sum([portions[i] for i in movable]), spare
        for i in movable:
            extra = min(most - counts[i], max(1, left * portions[i] // mass), spare)
            counts[i] = counts[i] + extra
            spare = spare - extra
    return np.array(counts)


def bell_draw(own_key, dims, deviation, reach, split=(), kind=jnp.bfloat16):
    drawn = jax.random.normal(own_key, dims, jnp.float32) * deviation
    if len(split) > 0:
        drawn = steps_of(own_key, dims, split, -0.22, 0.18) * drawn
    return jnp.clip(drawn, min=-reach, max=reach).astype(kind)


def setup_inputs(seed: int = 0) -> dict:
    seeds = jax.random.split(jax.random.key(seed), 14)
    tokens = bell_draw(seeds[0], (TOKENS, D), 1.0, 6.0, ((0, 32),))
    groups = jax.vmap(lambda own: jnp.searchsorted(jnp.cumsum(uneven(own, GROUPS_DEV, TOK_DEV, GROUP_LEN, 0)), jnp.arange(TOK_DEV), side="right"))(jax.random.split(seeds[1], DEVICES_ALL)).reshape((DEVICES_ALL, TOK_DEV)).astype(jnp.int32)
    key_mask = plant((jax.random.randint(seeds[2], (TOKENS,), 0, 8) < 7).astype(jnp.int32), jax.random.fold_in(seeds[2], 1), 0, 1)
    routes_keys = jax.random.split(jax.random.fold_in(seeds[3], 1), TOKENS // TOK_DEV)
    routes_turns = jax.random.permutation(jax.random.fold_in(seeds[3], 3), TOKENS // TOK_DEV)
    routes = jax.vmap(lambda own, number: shared_out(jax.random.fold_in(seeds[3], 2), own, number, TOK_DEV, EXPERTS, 1, MOST, 2))(routes_keys, routes_turns).reshape((TOKENS, 1))
    query_weight = bell_draw(seeds[4], (LAYERS, D, D), D ** -0.5, 0.21875, ((1, 32),))
    key_weight = bell_draw(seeds[5], (LAYERS, D, D), D ** -0.5, 0.21875, ((1, 32),))
    value_weight = bell_draw(seeds[6], (LAYERS, D, D), D ** -0.5, 0.21875, ((1, 32),))
    output_weight = bell_draw(seeds[7], (LAYERS, D, D), (D // 64) ** -0.5, 1.75, ((1, 32),))
    norm_first = jnp.clip(1.0 + 0.15 * jax.random.normal(seeds[8], (LAYERS, D), jnp.float32), 0.25, 1.75).astype(jnp.bfloat16)
    norm_second = jnp.clip(1.0 + 0.15 * jax.random.normal(seeds[9], (LAYERS, D), jnp.float32), 0.25, 1.75).astype(jnp.bfloat16)
    expert_in = bell_draw(seeds[10], (LAYERS, EXPERTS, D, FF), D ** -0.5, 0.21875, ((2, 8), (3, 4)))
    expert_out = bell_draw(seeds[11], (LAYERS, EXPERTS, FF, D), FF ** -0.5, 0.109375, ((2, 4), (3, 8)))
    cotangent = bell_draw(seeds[12], (TOKENS, D), 1.0, 6.0, ((0, 32),), jnp.float32)
    return dict(tokens=tokens, groups=groups, key_mask=key_mask, routes=routes, query_weight=query_weight, key_weight=key_weight, value_weight=value_weight, output_weight=output_weight, norm_first=norm_first, norm_second=norm_second, expert_in=expert_in, expert_out=expert_out, cotangent=cotangent)


@jax.custom_vjp
def low(v):
    return lax.optimization_barrier(v.astype(jnp.bfloat16)).astype(jnp.float32)

@jax.custom_vjp
def low_back(v):
    return v

def low_keep(v):
    return (low(v), None)

def low_pass(kept, grad):
    return (grad,)

def back_keep(v):
    return (v, None)

def back_low(kept, grad):
    return (low(grad),)
low.defvjp(low_keep, low_pass)
low_back.defvjp(back_keep, back_low)
epsilon = 1e-05
score_scale = 0.125
blocks_together = 8

def matmul(left, right):
    return jnp.dot(left, right, precision=lax.Precision.HIGHEST)

def layer_norm(values, gain_vector):
    average = lax.optimization_barrier(jnp.mean(values, -1, keepdims=True))
    centered = values - average
    spread = lax.optimization_barrier(jnp.mean(centered * centered, -1, keepdims=True))
    return centered * lax.rsqrt(spread + epsilon) * gain_vector

def slot_tables(route_row):
    row_count = route_row.shape[0]
    one_hot = (route_row[:, None] == jnp.arange(EXPERTS, dtype=jnp.int32)[None, :]).astype(jnp.int32)
    running = jnp.cumsum(one_hot, 0).astype(jnp.int32) - 1
    position = lax.optimization_barrier(jnp.sum(running * one_hot, 1)).astype(jnp.int32)
    slot_of = route_row * MOST + position
    token_of = jnp.zeros((EXPERTS * MOST,), jnp.int32).at[slot_of].set(jnp.arange(row_count, dtype=jnp.int32))
    filled = jnp.zeros((EXPERTS * MOST,), jnp.int32).at[slot_of].set(1)
    return (slot_of, token_of, filled)

def allowed_pairs(group_row, mask_row):
    row_count = group_row.shape[0]
    same_group = group_row[:, None] == group_row[None, :]
    diagonal = jnp.arange(row_count)[:, None] == jnp.arange(row_count)[None, :]
    return same_group & ((mask_row[None, :] == 1) | diagonal)

def one_layer(inputs, allowed, tables, params):
    query_weight, key_weight, value_weight, output_weight, first_gain, second_gain, weight_in, weight_out = params
    row_count = inputs.shape[0]
    normed = low(layer_norm(inputs, first_gain))
    query_rows = low_back(low(matmul(normed, query_weight)))
    key_rows = low_back(low(matmul(normed, key_weight)))
    value_rows = low_back(low(matmul(normed, value_weight)))

    def one_head(head_index):
        start = head_index * HEAD_DIM
        query_head = lax.dynamic_slice_in_dim(query_rows, start, HEAD_DIM, 1)
        key_head = lax.dynamic_slice_in_dim(key_rows, start, HEAD_DIM, 1)
        value_head = lax.dynamic_slice_in_dim(value_rows, start, HEAD_DIM, 1)
        scores = low_back(matmul(query_head, key_head.T) * score_scale)
        scores = jnp.where(allowed, scores, -1e+30)
        probs = jax.nn.softmax(scores, axis=-1)
        return matmul(low(probs), value_head)
    contexts = lax.map(jax.checkpoint(one_head), jnp.arange(HEADS, dtype=jnp.int32))
    context = jnp.transpose(contexts, (1, 0, 2)).reshape(row_count, HEADS * HEAD_DIM)
    context = low_back(low(context))
    hidden_in = inputs + low_back(matmul(context, output_weight))
    second = low(layer_norm(hidden_in, second_gain))
    slot_of, token_of, filled = tables
    slot_rows = jnp.where(filled[:, None] == 1, second[token_of], 0.0)
    grouped = slot_rows.reshape(EXPERTS, MOST, D)
    before = low_back(jnp.einsum('emc,ecf->emf', grouped, weight_in, precision=lax.Precision.HIGHEST))
    activated = low(jax.nn.gelu(before, approximate=False))
    produced = low_back(jnp.einsum('emf,efc->emc', activated, weight_out, precision=lax.Precision.HIGHEST))
    produced = produced.reshape(EXPERTS * MOST, D)
    return hidden_in + produced[slot_of]

def device_block(rows, group_row, mask_row, route_row, params):
    allowed = allowed_pairs(group_row, mask_row)
    tables = slot_tables(route_row)
    for layer_index in range(LAYERS):
        rows = one_layer(rows, allowed, tables, [weight[layer_index] for weight in params])
    return rows

def run_all(rows, params, groups, key_mask, routes):
    bundles = N_DP * N_EXPERT // blocks_together
    rows = rows.reshape(bundles, blocks_together, TOK_DEV, D)
    group_rows = groups.reshape(bundles, blocks_together, TOK_DEV)
    mask_rows = key_mask.reshape(bundles, blocks_together, TOK_DEV)
    route_rows = routes.reshape(bundles, blocks_together, TOK_DEV)

    def one_bundle(items):
        return jax.vmap(lambda r, g, m, t: device_block(r, g, m, t, params))(items[0], items[1], items[2], items[3])
    result = lax.map(jax.checkpoint(one_bundle), (rows, group_rows, mask_rows, route_rows))
    return result.reshape(TOKENS, D)

def reference(tokens, groups, key_mask, routes, query_weight, key_weight, value_weight, output_weight, norm_first, norm_second, expert_in, expert_out, cotangent):
    floats = [weight.astype(jnp.float32) for weight in (query_weight, key_weight, value_weight, output_weight, norm_first, norm_second, expert_in, expert_out)]
    start_rows = tokens.astype(jnp.float32)

    def forward(rows, *params):
        return run_all(rows, params, groups, key_mask, routes[:, 0])
    result, pullback = jax.vjp(forward, start_rows, *floats)
    grads = pullback(cotangent.astype(jnp.float32))
    return (result.astype(jnp.bfloat16), grads[0], grads[1], grads[2], grads[3], grads[4], grads[5], grads[6], grads[7], grads[8])
```

```python
from functools import partial

import jax
import jax.numpy as jnp
from jax import lax
from jax.experimental import pallas as pl
from jax.experimental.pallas import tpu as pltpu
from jax.sharding import PartitionSpec as P

HEADS = 12
HEAD_DIM = 64
EXPERTS = 3
LAYERS = 2
MOST = 144

SLOTS = EXPERTS * MOST
PAIR = 2 * HEAD_DIM
epsilon = 1e-05
score_scale = 0.125
FAR = -1e30
VMEM_BYTES = 56 << 20
f32 = jnp.float32
bf16 = jnp.bfloat16


def mat(left, right):
    return jnp.dot(left, right, preferred_element_type=f32)


def contract_rows(left, right):
    return lax.dot_general(left, right, (((0,), (0,)), ((), ())), preferred_element_type=f32)


def contract_cols(left, right):
    return lax.dot_general(left, right, (((1,), (1,)), ((), ())), preferred_element_type=f32)


def norm_parts(values):
    average = jnp.mean(values, -1, keepdims=True)
    centered = values - average
    spread = jnp.mean(centered * centered, -1, keepdims=True)
    rate = lax.rsqrt(spread + epsilon)
    return centered * rate, rate


def norm_back(unit, rate, scaled_grad):
    first = jnp.mean(scaled_grad, -1, keepdims=True)
    second = jnp.mean(scaled_grad * unit, -1, keepdims=True)
    return rate * (scaled_grad - first - unit * second)


def whole_call(body, out_shape, scratch_shapes=(), name=None):
    return pl.pallas_call(
        body,
        out_shape=out_shape,
        scratch_shapes=scratch_shapes,
        compiler_params=pltpu.CompilerParams(vmem_limit_bytes=VMEM_BYTES),
        name=name,
    )


def attend_forward_body(first, *refs):
    if first:
        rows_ref, spot_ref, bias_ref, gain_ref, weight_ref = refs[:5]
        outs = refs[5:]
        rows = rows_ref[...].astype(f32)
    else:
        rows_ref, part_a_ref, part_b_ref, spot_ref, bias_ref, gain_ref, weight_ref = refs[:7]
        outs = refs[7:]
        spot = spot_ref[...]
        rows = rows_ref[...] + mat(spot, part_a_ref[...]) + mat(spot, part_b_ref[...])
    width = rows.shape[1]
    triple_ref, logs_ref, context_ref, hidden_ref, slots_ref = outs[:5]
    if not first:
        outs[5][...] = rows
    unit, _ = norm_parts(rows)
    normed = (unit * gain_ref[0:1, :]).astype(bf16)
    triple_ref[...] = mat(normed, weight_ref[:, : 3 * width]).astype(bf16)
    row_count = rows.shape[0]
    lane = lax.broadcasted_iota(jnp.int32, (row_count, PAIR), 1)
    logs_ref[...] = jnp.zeros_like(logs_ref)

    def one_pair(pair, carry):
        at = pl.multiple_of(pair * PAIR, PAIR)
        query = triple_ref[:, pl.ds(at, PAIR)]
        key = triple_ref[:, pl.ds(at + width, PAIR)]
        value = triple_ref[:, pl.ds(at + 2 * width, PAIR)]
        sides = []
        logs = logs_ref[...]
        for side in range(2):
            mine = (lane >= HEAD_DIM) if side else (lane < HEAD_DIM)
            scores = contract_cols(jnp.where(mine, query, jnp.zeros((), bf16)), key)
            scores = scores * score_scale + bias_ref[...]
            highest = jnp.max(scores, 1, keepdims=True)
            powers = jnp.exp(scores - highest)
            totals = jnp.sum(powers, 1, keepdims=True)
            probs = (powers * (1.0 / totals)).astype(bf16)
            sides.append(mat(probs, value))
            logs = jnp.where(lane == 2 * pair + side, highest + jnp.log(totals), logs)
        logs_ref[...] = logs
        context_ref[:, pl.ds(at, PAIR)] = jnp.where(lane < HEAD_DIM, sides[0], sides[1]).astype(bf16)
        return carry

    lax.fori_loop(0, HEADS // 2, one_pair, 0)
    hidden = rows + mat(context_ref[...], weight_ref[:, 3 * width :])
    hidden_ref[...] = hidden
    unit, _ = norm_parts(hidden)
    second = (unit * gain_ref[1:2, :]).astype(bf16)
    slots_ref[...] = contract_rows(spot_ref[...], second).astype(bf16)


def attend_backward_body(last, *refs):
    (
        part_a_ref,
        part_b_ref,
        grad_ref,
        hidden_ref,
        rows_ref,
        triple_ref,
        logs_ref,
        context_ref,
        spot_ref,
        bias_ref,
        gain_ref,
        weight_ref,
    ) = refs[:12]
    if last:
        grad_out_ref, weight_grad_ref, context_grad_ref, triple_grad_ref = refs[12:]
        slots_ref = None
    else:
        grad_out_ref, weight_grad_ref, slots_ref, context_grad_ref, triple_grad_ref = refs[12:]
    spot = spot_ref[...]
    second_grad = mat(spot, part_a_ref[...]) + mat(spot, part_b_ref[...])
    unit, rate = norm_parts(hidden_ref[...])
    second_gain_grad = jnp.sum(second_grad * unit, 0, keepdims=True)
    hidden_grad = grad_ref[...] + norm_back(unit, rate, second_grad * gain_ref[1:2, :])
    row_count, width = hidden_grad.shape
    grad_out_ref[...] = hidden_grad
    branch = hidden_grad.astype(bf16)
    context_grad_ref[...] = contract_cols(branch, weight_ref[:, 3 * width :]).astype(bf16)
    weight_grad_ref[:, 3 * width : 4 * width] = contract_rows(context_ref[...], branch).astype(bf16)
    lane = lax.broadcasted_iota(jnp.int32, (row_count, PAIR), 1)

    def one_pair(pair, carry):
        at = pl.multiple_of(pair * PAIR, PAIR)
        query = triple_ref[:, pl.ds(at, PAIR)]
        key = triple_ref[:, pl.ds(at + width, PAIR)]
        value = triple_ref[:, pl.ds(at + 2 * width, PAIR)]
        gone = context_grad_ref[:, pl.ds(at, PAIR)]
        zero = jnp.zeros((), bf16)
        query_sides, key_sides, value_sides = [], [], []
        for side in range(2):
            mine = (lane >= HEAD_DIM) if side else (lane < HEAD_DIM)
            log_total = jnp.sum(
                jnp.where(lane == 2 * pair + side, logs_ref[...], 0.0), 1, keepdims=True
            )
            scores = contract_cols(jnp.where(mine, query, zero), key)
            scores = scores * score_scale + bias_ref[...]
            probs = jnp.exp(scores - log_total)
            prob_grad = contract_cols(jnp.where(mine, gone, zero), value)
            inner = jnp.sum(probs * prob_grad, 1, keepdims=True)
            score_grad = (probs * (prob_grad - inner)).astype(bf16)
            query_sides.append(mat(score_grad, key))
            key_sides.append(contract_rows(score_grad, query))
            value_sides.append(contract_rows(probs.astype(bf16), gone))
        left = lane < HEAD_DIM
        triple_grad_ref[:, pl.ds(at, PAIR)] = (
            score_scale * jnp.where(left, query_sides[0], query_sides[1])
        ).astype(bf16)
        triple_grad_ref[:, pl.ds(at + width, PAIR)] = (
            score_scale * jnp.where(left, key_sides[0], key_sides[1])
        ).astype(bf16)
        triple_grad_ref[:, pl.ds(at + 2 * width, PAIR)] = jnp.where(
            left, value_sides[0], value_sides[1]
        ).astype(bf16)
        return carry

    lax.fori_loop(0, HEADS // 2, one_pair, 0)
    unit, rate = norm_parts(rows_ref[...].astype(f32))
    normed = (unit * gain_ref[0:1, :]).astype(bf16)
    triple_grad = triple_grad_ref[...]
    weight_grad_ref[:, : 3 * width] = contract_rows(normed, triple_grad).astype(bf16)
    normed_grad = contract_cols(triple_grad, weight_ref[:, : 3 * width])
    first_gain_grad = jnp.sum(normed_grad * unit, 0, keepdims=True)
    out_grad = grad_out_ref[...] + norm_back(unit, rate, normed_grad * gain_ref[0:1, :])
    grad_out_ref[...] = out_grad
    if slots_ref is not None:
        slots_ref[...] = contract_rows(spot, out_grad.astype(bf16)).astype(bf16)
    which = lax.broadcasted_iota(jnp.int32, (PAIR, width), 0)
    gain_rows = jnp.where(
        which == 0, first_gain_grad, jnp.where(which == 1, second_gain_grad, 0.0)
    )
    weight_grad_ref[:, 4 * width :] = gain_rows.T.astype(bf16)


def expert_forward_body(*refs):
    block_refs, weight_ref = refs[:4], refs[4]
    out_refs, active_ref, slope_ref = refs[5:9], refs[9], refs[10]
    width = block_refs[0].shape[1]
    units = weight_ref.shape[1] // 2
    for half in range(2):
        rows = jnp.concatenate([block_refs[2 * half][...], block_refs[2 * half + 1][...]], 0)
        before = mat(rows, weight_ref[:, :units])
        share = 0.5 + 0.5 * lax.erf(before * 0.7071067811865476)
        slope = share + before * (0.3989422804014327 * jnp.exp(-0.5 * before * before))
        active = (before * share).astype(bf16)
        span = slice(half * 2 * MOST, (half + 1) * 2 * MOST)
        active_ref[span, :] = active
        slope_ref[span, :] = slope.astype(bf16)
        sums = contract_cols(active, weight_ref[:, units:]).astype(bf16)
        out_refs[2 * half][...] = sums[:MOST]
        out_refs[2 * half + 1][...] = sums[MOST:]


def expert_backward_body(*refs):
    grad_refs, block_refs = refs[:4], refs[4:8]
    active_ref, slope_ref, weight_ref = refs[8:11]
    out_refs, weight_grad_ref = refs[11:15], refs[15]
    units = weight_ref.shape[1] // 2
    grads = jnp.concatenate([ref[...] for ref in grad_refs], 0)
    rows = jnp.concatenate([ref[...] for ref in block_refs], 0)
    active_grad = mat(grads, weight_ref[:, units:])
    before_grad = (active_grad * slope_ref[...].astype(f32)).astype(bf16)
    sums = contract_cols(before_grad, weight_ref[:, :units]).astype(bf16)
    for place in range(4):
        out_refs[place][...] = sums[place * MOST : (place + 1) * MOST]
    weight_grad_ref[:, :units] = contract_rows(rows, before_grad).astype(bf16)
    weight_grad_ref[:, units:] = contract_rows(grads, active_ref[...]).astype(bf16)


def expert_forward(blocks, weights):
    width = blocks[0].shape[1]
    units = weights.shape[1] // (2 * EXPERTS)
    block = pl.BlockSpec((MOST, width), lambda e: (e, 0))
    kept = pl.BlockSpec((4 * MOST, units), lambda e: (e, 0))
    outs = pl.pallas_call(
        expert_forward_body,
        grid=(EXPERTS,),
        in_specs=[block] * 4 + [pl.BlockSpec((width, 2 * units), lambda e: (0, e))],
        out_specs=[block] * 4 + [kept] * 2,
        out_shape=[jax.ShapeDtypeStruct((SLOTS, width), bf16)] * 4
        + [jax.ShapeDtypeStruct((4 * SLOTS, units), bf16)] * 2,
        compiler_params=pltpu.CompilerParams(vmem_limit_bytes=VMEM_BYTES),
        name="expert_forward",
    )(*blocks, weights)
    return outs[:4], outs[4], outs[5]


def expert_backward(grads, blocks, active, slope, weights):
    width = blocks[0].shape[1]
    units = weights.shape[1] // (2 * EXPERTS)
    block = pl.BlockSpec((MOST, width), lambda e: (e, 0))
    kept = pl.BlockSpec((4 * MOST, units), lambda e: (e, 0))
    square = pl.BlockSpec((width, 2 * units), lambda e: (0, e))
    outs = pl.pallas_call(
        expert_backward_body,
        grid=(EXPERTS,),
        in_specs=[block] * 8 + [kept] * 2 + [square],
        out_specs=[block] * 4 + [square],
        out_shape=[jax.ShapeDtypeStruct((SLOTS, width), bf16)] * 4
        + [jax.ShapeDtypeStruct(weights.shape, bf16)],
        compiler_params=pltpu.CompilerParams(vmem_limit_bytes=VMEM_BYTES),
        name="expert_backward",
    )(*grads, *blocks, active, slope, weights)
    return outs[:4], outs[4]


def swap(values, flip):
    count = lax.axis_size("expert")
    return lax.ppermute(values, "expert", [(i, i ^ flip) for i in range(count)])


def spread_slots(slots):
    across = swap(slots, 2)
    beside = swap(slots, 1)
    corner = swap(across, 1)
    return [slots, beside, across, corner]


def collect_slots(parts):
    own, beside, across, corner = parts
    corner_in = swap(corner, 1)
    beside_in = swap(beside, 1)
    far = (across.astype(f32) + corner_in.astype(f32)).astype(bf16)
    far_in = swap(far, 2)
    near = (own.astype(f32) + beside_in.astype(f32)).astype(bf16)
    return near, far_in


def on_device(
    tokens,
    groups,
    key_mask,
    routes,
    query_weight,
    key_weight,
    value_weight,
    output_weight,
    norm_first,
    norm_second,
    expert_in,
    expert_out,
    cotangent,
):
    both = ("dp", "expert")
    row_count, width = tokens.shape
    units = expert_in.shape[3]
    shard_rows = expert_in.shape[2]
    own_rows = query_weight.shape[1]

    gains = jnp.stack([norm_first[0], norm_second[0], norm_first[1], norm_second[1]], 1)
    gains = jnp.pad(gains, ((0, 0), (0, PAIR - gains.shape[1])))
    attention_shard = jnp.concatenate(
        [
            weight[layer]
            for layer in range(LAYERS)
            for weight in (query_weight, key_weight, value_weight, output_weight)
        ]
        + [gains],
        1,
    )
    attention_all = lax.all_gather(attention_shard, both, axis=0, tiled=True)
    gain_rows = attention_all[:, 4 * LAYERS * width :].T.astype(f32)

    def expert_shard(layer):
        pieces = jnp.concatenate(
            [expert_in[layer], jnp.transpose(expert_out[layer], (0, 2, 1))], 2
        )
        return jnp.transpose(pieces, (1, 0, 2)).reshape(shard_rows, EXPERTS * 2 * units)

    experts_all = [
        lax.all_gather(expert_shard(layer), "dp", axis=0, tiled=True) for layer in range(LAYERS)
    ]

    route = routes[:, 0]
    place = jnp.arange(row_count, dtype=jnp.int32)
    earlier = (route[:, None] == route[None, :]) & (place[None, :] < place[:, None])
    slot_of = route * MOST + jnp.sum(earlier.astype(jnp.int32), 1)
    spot = (slot_of[:, None] == jnp.arange(SLOTS, dtype=jnp.int32)[None, :]).astype(bf16)
    group = groups[0]
    allowed = (group[:, None] == group[None, :]) & (
        (key_mask[None, :] == 1) | (place[:, None] == place[None, :])
    )
    bias = jnp.where(allowed, 0.0, FAR).astype(f32)

    last_grads = spread_slots(contract_rows(spot, cotangent.astype(bf16)).astype(bf16))

    def shape_of(rows, cols, kind):
        return jax.ShapeDtypeStruct((rows, cols), kind)

    saved = []
    rows = tokens
    parts = None
    for layer in range(LAYERS):
        first = layer == 0
        weight = attention_all[:, 4 * layer * width : 4 * (layer + 1) * width]
        gain = gain_rows[2 * layer : 2 * layer + 2]
        outs = whole_call(
            partial(attend_forward_body, first),
            [
                shape_of(row_count, 3 * width, bf16),
                shape_of(row_count, PAIR, f32),
                shape_of(row_count, width, bf16),
                shape_of(row_count, width, f32),
                shape_of(SLOTS, width, bf16),
            ]
            + ([] if first else [shape_of(row_count, width, f32)]),
            name="attend_forward",
        )(*([rows] if first else [rows, *parts]), spot, bias, gain, weight)
        triple, logs, context, hidden, slots = outs[:5]
        inputs = tokens if first else outs[5]
        blocks = spread_slots(slots)
        sums, active, slope = expert_forward(blocks, experts_all[layer])
        parts = collect_slots(sums)
        rows = hidden
        saved.append((inputs, triple, logs, context, hidden, blocks, active, slope, weight, gain))
    mixed = (rows + mat(spot, parts[0]) + mat(spot, parts[1])).astype(bf16)

    grad = cotangent
    grad_blocks = last_grads
    results = [None] * LAYERS
    for layer in reversed(range(LAYERS)):
        inputs, triple, logs, context, hidden, blocks, active, slope, weight, gain = saved[layer]
        last = layer == 0
        sums, expert_grad = expert_backward(
            grad_blocks, blocks, active, slope, experts_all[layer]
        )
        expert_total = lax.psum_scatter(expert_grad, "dp", scatter_dimension=0, tiled=True)
        parts = collect_slots(sums)
        outs = whole_call(
            partial(attend_backward_body, last),
            [
                shape_of(row_count, width, f32),
                shape_of(width, 4 * width + PAIR, bf16),
            ]
            + ([] if last else [shape_of(SLOTS, width, bf16)]),
            scratch_shapes=[
                pltpu.VMEM((row_count, width), bf16),
                pltpu.VMEM((row_count, 3 * width), bf16),
            ],
            name="attend_backward",
        )(*parts, grad, hidden, inputs, triple, logs, context, spot, bias, gain, weight)
        grad, attention_grad = outs[:2]
        attention_total = lax.psum_scatter(attention_grad, both, scatter_dimension=0, tiled=True)
        if not last:
            grad_blocks = spread_slots(outs[2])
        results[layer] = (attention_total, expert_total)

    def columns(layer, start, stop):
        return results[layer][0][:, start:stop].astype(f32)

    deltas = [
        jnp.stack([columns(layer, i * width, (i + 1) * width) for layer in range(LAYERS)])
        for i in range(4)
    ]
    gain_deltas = [
        jnp.stack([columns(layer, 4 * width + i, 4 * width + i + 1)[:, 0] for layer in range(LAYERS)])
        for i in range(2)
    ]
    pieces = [
        results[layer][1].reshape(shard_rows, EXPERTS, 2, units).astype(f32)
        for layer in range(LAYERS)
    ]
    delta_in = jnp.stack([jnp.transpose(piece[:, :, 0], (1, 0, 2)) for piece in pieces])
    delta_out = jnp.stack([jnp.transpose(piece[:, :, 1], (1, 2, 0)) for piece in pieces])
    return (mixed, grad, *deltas, *gain_deltas, delta_in, delta_out)


def solution(mesh):
    placed = (
        P(("dp", "expert"), None),
        P(("dp", "expert"), None),
        P(("dp", "expert")),
        P(("dp", "expert"), None),
        P(None, ("dp", "expert"), None),
        P(None, ("dp", "expert"), None),
        P(None, ("dp", "expert"), None),
        P(None, ("dp", "expert"), None),
        P(None, ("dp", "expert")),
        P(None, ("dp", "expert")),
        P(None, None, "dp", "expert"),
        P(None, None, "expert", "dp"),
        P(("dp", "expert"), None),
    )
    return jax.shard_map(
        on_device,
        mesh=mesh,
        in_specs=placed,
        out_specs=(
            P(("dp", "expert"), None),
            P(("dp", "expert"), None),
            P(None, ("dp", "expert"), None),
            P(None, ("dp", "expert"), None),
            P(None, ("dp", "expert"), None),
            P(None, ("dp", "expert"), None),
            P(None, ("dp", "expert")),
            P(None, ("dp", "expert")),
            P(None, None, "dp", "expert"),
            P(None, None, "expert", "dp"),
        ),
        check_vma=False,
    )
```

```python
from functools import partial

import jax
import jax.numpy as jnp
from jax import lax
from jax.experimental import pallas as pl
from jax.experimental.pallas import tpu as pltpu
from jax.sharding import PartitionSpec as P

HEADS = 12
HEAD_DIM = 64
EXPERTS = 3
LAYERS = 2
MOST = 144

SLOTS = EXPERTS * MOST
PAIR = 2 * HEAD_DIM
epsilon = 1e-05
score_scale = 0.125
FAR = -1e30
RING_MOST = 8
VMEM_BYTES = 56 << 20
f32 = jnp.float32
bf16 = jnp.bfloat16


def mat(left, right):
    return jnp.dot(left, right, preferred_element_type=f32)


def contract_rows(left, right):
    return lax.dot_general(left, right, (((0,), (0,)), ((), ())), preferred_element_type=f32)


def contract_cols(left, right):
    return lax.dot_general(left, right, (((1,), (1,)), ((), ())), preferred_element_type=f32)


def norm_parts(values):
    average = jnp.mean(values, -1, keepdims=True)
    centered = values - average
    spread = jnp.mean(centered * centered, -1, keepdims=True)
    rate = lax.rsqrt(spread + epsilon)
    return centered * rate, rate


def norm_back(unit, rate, scaled_grad):
    first = jnp.mean(scaled_grad, -1, keepdims=True)
    second = jnp.mean(scaled_grad * unit, -1, keepdims=True)
    return rate * (scaled_grad - first - unit * second)


def cost(micros):
    return pl.CostEstimate(
        flops=micros * 10**5, transcendentals=0, bytes_accessed=micros * 10**2
    )


def whole_call(body, out_shape, scratch_shapes=(), name=None, micros=15):
    return pl.pallas_call(
        body,
        out_shape=out_shape,
        scratch_shapes=scratch_shapes,
        compiler_params=pltpu.CompilerParams(vmem_limit_bytes=VMEM_BYTES),
        cost_estimate=cost(micros),
        name=name,
    )


def pack_body(*refs):
    weight_refs, gain_refs, out_refs = refs[:4], refs[4:6], refs[6:]
    rows, width = weight_refs[0].shape[1:]
    lane = lax.broadcasted_iota(jnp.int32, (rows, PAIR), 1)
    diagonal = lax.broadcasted_iota(jnp.int32, (rows, rows), 0) == lax.broadcasted_iota(
        jnp.int32, (rows, rows), 1
    )
    for layer, out_ref in enumerate(out_refs):
        for place, weight_ref in enumerate(weight_refs):
            out_ref[:, place * width : (place + 1) * width] = weight_ref[layer]
        columns = [
            jnp.sum(jnp.where(diagonal, ref[layer : layer + 1, :].astype(f32), 0.0), 1, keepdims=True)
            for ref in gain_refs
        ]
        out_ref[:, 4 * width :] = jnp.where(
            lane == 0, columns[0], jnp.where(lane == 1, columns[1], 0.0)
        ).astype(bf16)


def attend_forward_body(first, *refs):
    if first:
        rows_ref, spot_ref, bias_ref, weight_ref = refs[:4]
        outs = refs[4:]
        rows = rows_ref[...].astype(f32)
    else:
        rows_ref, part_a_ref, part_b_ref, spot_ref, bias_ref, weight_ref = refs[:6]
        outs = refs[6:]
        spot = spot_ref[...]
        rows = rows_ref[...] + mat(spot, part_a_ref[...]) + mat(spot, part_b_ref[...])
    width = rows.shape[1]
    gains = weight_ref[:, 4 * width :].astype(f32).T
    triple_ref, logs_ref, context_ref, hidden_ref, slots_ref = outs[:5]
    if not first:
        outs[5][...] = rows
    unit, _ = norm_parts(rows)
    normed = (unit * gains[0:1, :]).astype(bf16)
    triple_ref[...] = mat(normed, weight_ref[:, : 3 * width]).astype(bf16)
    row_count = rows.shape[0]
    lane = lax.broadcasted_iota(jnp.int32, (row_count, PAIR), 1)
    logs_ref[...] = jnp.zeros_like(logs_ref)

    def one_pair(pair, carry):
        at = pl.multiple_of(pair * PAIR, PAIR)
        query = triple_ref[:, pl.ds(at, PAIR)]
        key = triple_ref[:, pl.ds(at + width, PAIR)]
        value = triple_ref[:, pl.ds(at + 2 * width, PAIR)]
        sides = []
        logs = logs_ref[...]
        for side in range(2):
            mine = (lane >= HEAD_DIM) if side else (lane < HEAD_DIM)
            scores = contract_cols(jnp.where(mine, query, jnp.zeros((), bf16)), key)
            scores = scores * score_scale + bias_ref[...]
            highest = jnp.max(scores, 1, keepdims=True)
            powers = jnp.exp(scores - highest)
            totals = jnp.sum(powers, 1, keepdims=True)
            probs = (powers * (1.0 / totals)).astype(bf16)
            sides.append(mat(probs, value))
            logs = jnp.where(lane == 2 * pair + side, highest + jnp.log(totals), logs)
        logs_ref[...] = logs
        context_ref[:, pl.ds(at, PAIR)] = jnp.where(lane < HEAD_DIM, sides[0], sides[1]).astype(bf16)
        return carry

    lax.fori_loop(0, HEADS // 2, one_pair, 0)
    hidden = rows + mat(context_ref[...], weight_ref[:, 3 * width : 4 * width])
    hidden_ref[...] = hidden
    unit, _ = norm_parts(hidden)
    second = (unit * gains[1:2, :]).astype(bf16)
    slots_ref[...] = contract_rows(spot_ref[...], second).astype(bf16)


def attend_backward_body(last, *refs):
    (
        part_a_ref,
        part_b_ref,
        grad_ref,
        hidden_ref,
        rows_ref,
        triple_ref,
        logs_ref,
        context_ref,
        spot_ref,
        bias_ref,
        weight_ref,
    ) = refs[:11]
    slots_ref = None
    if last:
        grad_out_ref, first_grad_ref, second_grad_ref, context_grad_ref, triple_grad_ref = refs[11:]
    else:
        grad_out_ref, first_grad_ref, slots_ref, context_grad_ref, triple_grad_ref = refs[11:]
    width = rows_ref.shape[1]
    gains = weight_ref[:, 4 * width :].astype(f32).T
    spot = spot_ref[...]
    second_grad = mat(spot, part_a_ref[...]) + mat(spot, part_b_ref[...])
    unit, rate = norm_parts(hidden_ref[...])
    second_gain_grad = jnp.sum(second_grad * unit, 0, keepdims=True)
    hidden_grad = grad_ref[...] + norm_back(unit, rate, second_grad * gains[1:2, :])
    row_count, width = hidden_grad.shape
    grad_out_ref[...] = hidden_grad
    branch = hidden_grad.astype(bf16)
    context_grad_ref[...] = contract_cols(branch, weight_ref[:, 3 * width : 4 * width]).astype(bf16)
    output_grad = contract_rows(context_ref[...], branch).astype(bf16)
    if last:
        second_grad_ref[:, width : 2 * width] = output_grad
    else:
        first_grad_ref[:, 3 * width : 4 * width] = output_grad
    lane = lax.broadcasted_iota(jnp.int32, (row_count, PAIR), 1)

    def one_pair(pair, carry):
        at = pl.multiple_of(pair * PAIR, PAIR)
        query = triple_ref[:, pl.ds(at, PAIR)]
        key = triple_ref[:, pl.ds(at + width, PAIR)]
        value = triple_ref[:, pl.ds(at + 2 * width, PAIR)]
        gone = context_grad_ref[:, pl.ds(at, PAIR)]
        zero = jnp.zeros((), bf16)
        query_sides, key_sides, value_sides = [], [], []
        for side in range(2):
            mine = (lane >= HEAD_DIM) if side else (lane < HEAD_DIM)
            log_total = jnp.sum(
                jnp.where(lane == 2 * pair + side, logs_ref[...], 0.0), 1, keepdims=True
            )
            scores = contract_cols(jnp.where(mine, query, zero), key)
            scores = scores * score_scale + bias_ref[...]
            probs = jnp.exp(scores - log_total)
            prob_grad = contract_cols(jnp.where(mine, gone, zero), value)
            inner = jnp.sum(probs * prob_grad, 1, keepdims=True)
            score_grad = (probs * (prob_grad - inner)).astype(bf16)
            query_sides.append(mat(score_grad, key))
            key_sides.append(contract_rows(score_grad, query))
            value_sides.append(contract_rows(probs.astype(bf16), gone))
        left = lane < HEAD_DIM
        triple_grad_ref[:, pl.ds(at, PAIR)] = (
            score_scale * jnp.where(left, query_sides[0], query_sides[1])
        ).astype(bf16)
        triple_grad_ref[:, pl.ds(at + width, PAIR)] = (
            score_scale * jnp.where(left, key_sides[0], key_sides[1])
        ).astype(bf16)
        triple_grad_ref[:, pl.ds(at + 2 * width, PAIR)] = jnp.where(
            left, value_sides[0], value_sides[1]
        ).astype(bf16)
        return carry

    lax.fori_loop(0, HEADS // 2, one_pair, 0)
    unit, rate = norm_parts(rows_ref[...].astype(f32))
    normed = (unit * gains[0:1, :]).astype(bf16)
    triple_grad = triple_grad_ref[...]
    if last:
        first_grad_ref[...] = contract_rows(normed, triple_grad[:, : 2 * width]).astype(bf16)
        second_grad_ref[:, :width] = contract_rows(normed, triple_grad[:, 2 * width :]).astype(bf16)
    else:
        first_grad_ref[:, : 3 * width] = contract_rows(normed, triple_grad).astype(bf16)
    normed_grad = contract_cols(triple_grad, weight_ref[:, : 3 * width])
    first_gain_grad = jnp.sum(normed_grad * unit, 0, keepdims=True)
    out_grad = grad_out_ref[...] + norm_back(unit, rate, normed_grad * gains[0:1, :])
    grad_out_ref[...] = out_grad
    if slots_ref is not None:
        slots_ref[...] = contract_rows(spot, out_grad.astype(bf16)).astype(bf16)
    which = lax.broadcasted_iota(jnp.int32, (PAIR, width), 0)
    gain_rows = jnp.where(
        which == 0, first_gain_grad, jnp.where(which == 1, second_gain_grad, 0.0)
    )
    if last:
        second_grad_ref[:, 2 * width :] = gain_rows.T.astype(bf16)
    else:
        first_grad_ref[:, 4 * width :] = gain_rows.T.astype(bf16)


def expert_forward_body(*refs):
    block_refs, weight_ref = refs[:4], refs[4]
    out_refs, active_ref, slope_ref = refs[5:9], refs[9], refs[10]
    width = block_refs[0].shape[1]
    units = weight_ref.shape[1] // 2
    for half in range(2):
        rows = jnp.concatenate([block_refs[2 * half][...], block_refs[2 * half + 1][...]], 0)
        before = mat(rows, weight_ref[:, :units])
        share = 0.5 + 0.5 * lax.erf(before * 0.7071067811865476)
        slope = share + before * (0.3989422804014327 * jnp.exp(-0.5 * before * before))
        active = (before * share).astype(bf16)
        span = slice(half * 2 * MOST, (half + 1) * 2 * MOST)
        active_ref[span, :] = active
        slope_ref[span, :] = slope.astype(bf16)
        sums = contract_cols(active, weight_ref[:, units:]).astype(bf16)
        out_refs[2 * half][...] = sums[:MOST]
        out_refs[2 * half + 1][...] = sums[MOST:]


def expert_backward_body(split, *refs):
    if split:
        place_ref, *refs = refs
    grad_refs, block_refs = refs[:4], refs[4:8]
    active_ref, slope_ref, weight_ref = refs[8:11]
    out_refs = refs[11:15]
    units = weight_ref.shape[1] // 2
    grads = jnp.concatenate([ref[...] for ref in grad_refs], 0)
    rows = jnp.concatenate([ref[...] for ref in block_refs], 0)
    active_grad = mat(grads, weight_ref[:, units:])
    before_grad = (active_grad * slope_ref[...].astype(f32)).astype(bf16)
    sums = contract_cols(before_grad, weight_ref[:, :units]).astype(bf16)
    for place in range(4):
        out_refs[place][...] = sums[place * MOST : (place + 1) * MOST]
    pieces = ((rows, before_grad, 0), (grads, active_ref[...], units))
    if not split:
        for left, right, start in pieces:
            refs[15][:, start : start + units] = contract_rows(left, right).astype(bf16)
        return
    ring, mine = place_ref[0], place_ref[1]
    outer, count = refs[15].shape[:2]
    for left, right, start in pieces:
        grad = contract_rows(left, right).astype(bf16)
        for expert in range(EXPERTS):
            kept_ref, sent_ref = refs[15 + 2 * expert], refs[16 + 2 * expert]
            for half in range(2):

                @pl.when((pl.program_id(0) == expert) & (mine == half))
                def _():
                    for block in range(outer):
                        at = lax.rem(block - ring + outer, outer)
                        low = (2 * block + half) * count
                        high = (2 * block + 1 - half) * count
                        kept_ref[at, :, start : start + units] = grad[low : low + count]
                        sent_ref[at, :, start : start + units] = grad[high : high + count]


def expert_forward(blocks, weights):
    width = blocks[0].shape[1]
    units = weights.shape[1] // (2 * EXPERTS)
    block = pl.BlockSpec((MOST, width), lambda e: (e, 0))
    kept = pl.BlockSpec((4 * MOST, units), lambda e: (e, 0))
    outs = pl.pallas_call(
        expert_forward_body,
        grid=(EXPERTS,),
        in_specs=[block] * 4 + [pl.BlockSpec((width, 2 * units), lambda e: (0, e))],
        out_specs=[block] * 4 + [kept] * 2,
        out_shape=[jax.ShapeDtypeStruct((SLOTS, width), bf16)] * 4
        + [jax.ShapeDtypeStruct((4 * SLOTS, units), bf16)] * 2,
        compiler_params=pltpu.CompilerParams(vmem_limit_bytes=VMEM_BYTES),
        cost_estimate=cost(10),
        name="expert_forward",
    )(*blocks, weights)
    return outs[:4], outs[4], outs[5]


def expert_backward(grads, blocks, active, slope, weights, split):
    width = blocks[0].shape[1]
    units = weights.shape[1] // (2 * EXPERTS)
    block = pl.BlockSpec((MOST, width), lambda e, *_: (e, 0))
    kept = pl.BlockSpec((4 * MOST, units), lambda e, *_: (e, 0))
    square = pl.BlockSpec((width, 2 * units), lambda e, *_: (0, e))
    out_specs = [block] * 4
    out_shape = [jax.ShapeDtypeStruct((SLOTS, width), bf16)] * 4
    places = []
    if split:
        count = lax.axis_size("dp")
        me = lax.axis_index("dp")
        places = [jnp.stack([me // 2, lax.rem(me, 2)]).astype(jnp.int32)]
        shape = (count // 2, width // count, 2 * units)
        out_specs += [pl.BlockSpec(shape, lambda e, *_: (0, 0, 0))] * (2 * EXPERTS)
        out_shape += [jax.ShapeDtypeStruct(shape, bf16)] * (2 * EXPERTS)
    else:
        out_specs += [square]
        out_shape += [jax.ShapeDtypeStruct(weights.shape, bf16)]
    outs = pl.pallas_call(
        partial(expert_backward_body, split),
        grid_spec=pltpu.PrefetchScalarGridSpec(
            num_scalar_prefetch=len(places),
            grid=(EXPERTS,),
            in_specs=[block] * 8 + [kept] * 2 + [square],
            out_specs=out_specs,
        ),
        out_shape=out_shape,
        compiler_params=pltpu.CompilerParams(vmem_limit_bytes=VMEM_BYTES),
        cost_estimate=cost(16),
        name="expert_backward",
    )(*places, *grads, *blocks, active, slope, weights)
    return outs[:4], outs[4:]


def swap(values, flip):
    count = lax.axis_size("expert")
    return lax.ppermute(values, "expert", [(i, i ^ flip) for i in range(count)])


def spread_slots(slots):
    across = swap(slots, 2)
    beside = swap(slots, 1)
    corner = swap(across, 1)
    return [slots, beside, across, corner]


def collect_slots(parts):
    own, beside, across, corner = parts
    corner_in = swap(corner, 1)
    beside_in = swap(beside, 1)
    far = (across.astype(f32) + corner_in.astype(f32)).astype(bf16)
    far_in = swap(far, 2)
    near = (own.astype(f32) + beside_in.astype(f32)).astype(bf16)
    return near, far_in


def pair_perm(count):
    return [(i, i ^ 1) for i in range(count)]


def ring_perm(count):
    return [(i, (i + 2) % count) for i in range(count)]


def gather_rows(shard, line_done, pair_done):
    count = lax.axis_size("dp")
    if count > RING_MOST:
        return lax.all_gather(shard, "dp", axis=0, tiled=True)
    me = lax.axis_index("dp")
    rows, cols = shard.shape
    full = jnp.zeros((count * rows, cols), shard.dtype)
    moving, _ = tie(shard, line_done)
    for step in range(count // 2):
        source = lax.rem(me - 2 * step + count, count)
        mate, _ = tie(moving, pair_done) if step == 0 else (moving, None)
        mate = lax.ppermute(mate, "dp", pair_perm(count))
        full = lax.dynamic_update_slice(full, moving, (source * rows, 0))
        full = lax.dynamic_update_slice(full, mate, ((source ^ 1) * rows, 0))
        if step + 1 < count // 2:
            moving = lax.ppermute(moving, "dp", ring_perm(count))
    return full


def tie(*values):
    return lax.optimization_barrier(values)


def add(left, right):
    return left.astype(f32) + right.astype(f32)


def pick(values, at, axis):
    return lax.dynamic_index_in_dim(values, at, axis, keepdims=False)


def put(values, piece, at, axis):
    return lax.dynamic_update_index_in_dim(values, piece, at, axis)


def shift_perm(count, step):
    return [(i, (i + 2 * step) % count) for i in range(count)]


def gather_attention(shard):
    count, sides = lax.axis_size("dp"), lax.axis_size("expert")
    if count > RING_MOST:
        return lax.all_gather(shard, ("dp", "expert"), axis=0, tiled=True), None, None
    rows, cols = shard.shape
    outer = count // 2
    me, side = lax.axis_index("dp"), lax.axis_index("expert")
    line = me // 2
    quad = put(jnp.zeros((outer, rows, cols), shard.dtype), shard, line, 0)
    for step in range(1, outer):
        got = lax.ppermute(shard, "dp", shift_perm(count, step))
        quad = put(quad, got, lax.rem(line - step + outer, outer), 0)
    mate = lax.ppermute(quad, "dp", pair_perm(count))
    both = jnp.zeros((outer, 2, rows, cols), shard.dtype)
    both = put(put(both, quad, lax.rem(me, 2), 1), mate, 1 - lax.rem(me, 2), 1)
    across = swap(both, 2)
    full = jnp.zeros((outer, 2, sides, rows, cols), shard.dtype)
    full = put(full, both, side, 2)
    full = put(full, swap(both, 1), side ^ 1, 2)
    full = put(full, across, side ^ 2, 2)
    full = put(full, swap(across, 1), side ^ 3, 2)
    return full.reshape(-1, cols), got, mate


def reduce_pairs(kept, got):
    count = lax.axis_size("dp")
    outer = count // 2
    total = add(kept[0], got[0])
    for step in range(1, outer):
        sent = add(kept[step], got[step]).astype(bf16)
        total = total + lax.ppermute(sent, "dp", shift_perm(count, step)).astype(f32)
    return total


def halve_core(blocks, axis):
    core = lax.rem(lax.axis_index("expert"), 2)
    got = swap(pick(blocks, 1 - core, axis), 1)
    return add(pick(blocks, core, axis), got).astype(bf16)


def halve_line(blocks, axis):
    line = lax.axis_index("expert") // 2
    got = swap(pick(blocks, 1 - line, axis), 2)
    return add(pick(blocks, line, axis), got).astype(bf16)


def halve_pair(blocks, axis):
    mine = lax.rem(lax.axis_index("dp"), 2)
    got = lax.ppermute(pick(blocks, 1 - mine, axis), "dp", pair_perm(lax.axis_size("dp")))
    return add(pick(blocks, mine, axis), got).astype(bf16)


def reduce_line(blocks):
    count = lax.axis_size("dp")
    outer = count // 2
    line = lax.axis_index("dp") // 2
    total = pick(blocks, line, 0).astype(f32)
    for step in range(1, outer):
        sent = pick(blocks, lax.rem(line + step, outer), 0)
        total = total + lax.ppermute(sent, "dp", shift_perm(count, step)).astype(f32)
    return total


def reduce_attention(values, pair_first, after=None):
    dp, sides = lax.axis_size("dp"), lax.axis_size("expert")
    cols = values.shape[1]
    if dp > RING_MOST:
        return lax.psum_scatter(values, ("dp", "expert"), scatter_dimension=0, tiled=True).astype(f32)
    blocks = halve_core(values.reshape(dp // 2, 2, sides // 2, 2, -1, cols), 3)
    if after is not None:
        blocks, _ = tie(blocks, after)
    if pair_first:
        blocks = halve_line(halve_pair(blocks, 1), 1)
    else:
        blocks = halve_pair(halve_line(blocks, 2), 1)
    return reduce_line(blocks)


def on_device(
    tokens,
    groups,
    key_mask,
    routes,
    query_weight,
    key_weight,
    value_weight,
    output_weight,
    norm_first,
    norm_second,
    expert_in,
    expert_out,
    cotangent,
):
    both = ("dp", "expert")
    row_count, width = tokens.shape
    units = expert_in.shape[3]
    shard_rows = expert_in.shape[2]
    own_rows = query_weight.shape[1]

    attention_shards = whole_call(
        pack_body,
        [jax.ShapeDtypeStruct((own_rows, 4 * width + PAIR), bf16)] * LAYERS,
        name="pack_attention",
    )(query_weight, key_weight, value_weight, output_weight, norm_first, norm_second)

    def expert_shard(layer):
        pieces = jnp.concatenate(
            [expert_in[layer], jnp.transpose(expert_out[layer], (0, 2, 1))], 2
        )
        return jnp.transpose(pieces, (1, 0, 2)).reshape(shard_rows, EXPERTS * 2 * units)

    attention_first, line_done, pair_done = gather_attention(attention_shards[0])
    attention_all = [
        attention_first,
        lax.all_gather(attention_shards[1], both, axis=0, tiled=True),
    ]
    experts_all = [
        gather_rows(expert_shard(0), line_done, pair_done),
        lax.all_gather(expert_shard(1), "dp", axis=0, tiled=True),
    ]

    route = routes[:, 0]
    place = jnp.arange(row_count, dtype=jnp.int32)
    earlier = (route[:, None] == route[None, :]) & (place[None, :] < place[:, None])
    slot_of = route * MOST + jnp.sum(earlier.astype(jnp.int32), 1)
    spot = (slot_of[:, None] == jnp.arange(SLOTS, dtype=jnp.int32)[None, :]).astype(bf16)
    group = groups[0]
    allowed = (group[:, None] == group[None, :]) & (
        (key_mask[None, :] == 1) | (place[:, None] == place[None, :])
    )
    bias = jnp.where(allowed, 0.0, FAR).astype(f32)

    last_grads = spread_slots(contract_rows(spot, cotangent.astype(bf16)).astype(bf16))

    def shape_of(rows, cols, kind):
        return jax.ShapeDtypeStruct((rows, cols), kind)

    saved = []
    rows = tokens
    parts = None
    for layer in range(LAYERS):
        first = layer == 0
        weight = attention_all[layer]
        outs = whole_call(
            partial(attend_forward_body, first),
            [
                shape_of(row_count, 3 * width, bf16),
                shape_of(row_count, PAIR, f32),
                shape_of(row_count, width, bf16),
                shape_of(row_count, width, f32),
                shape_of(SLOTS, width, bf16),
            ]
            + ([] if first else [shape_of(row_count, width, f32)]),
            name="attend_forward",
        )(*([rows] if first else [rows, *parts]), spot, bias, weight)
        triple, logs, context, hidden, slots = outs[:5]
        inputs = tokens if first else outs[5]
        blocks = spread_slots(slots)
        sums, active, slope = expert_forward(blocks, experts_all[layer])
        parts = collect_slots(sums)
        rows = hidden
        saved.append((inputs, triple, logs, context, hidden, blocks, active, slope, weight))
    mixed = (rows + mat(spot, parts[0]) + mat(spot, parts[1])).astype(bf16)

    grad = cotangent
    grad_blocks = last_grads
    results = [None] * LAYERS
    for layer in reversed(range(LAYERS)):
        inputs, triple, logs, context, hidden, blocks, active, slope, weight = saved[layer]
        last = layer == 0
        sums, expert_grads = expert_backward(
            grad_blocks, blocks, active, slope, experts_all[layer], False
        )
        total = lax.psum_scatter(expert_grads[0], "dp", scatter_dimension=0, tiled=True)
        total = total.astype(f32).reshape(shard_rows, EXPERTS, 2 * units)
        expert_totals = [total[:, expert] for expert in range(EXPERTS)]
        parts = collect_slots(sums)
        grad_widths = [2 * width, 2 * width + PAIR] if last else [4 * width + PAIR]
        outs = whole_call(
            partial(attend_backward_body, last),
            [shape_of(row_count, width, f32)]
            + [shape_of(width, cols, bf16) for cols in grad_widths]
            + ([] if last else [shape_of(SLOTS, width, bf16)]),
            scratch_shapes=[
                pltpu.VMEM((row_count, width), bf16),
                pltpu.VMEM((row_count, 3 * width), bf16),
            ],
            name="attend_backward",
        )(*parts, grad, hidden, inputs, triple, logs, context, spot, bias, weight)
        grad = outs[0]
        if last:
            attention_total = jnp.concatenate(
                [reduce_attention(outs[1], False), reduce_attention(outs[2], True)], 1
            )
        else:
            grad_blocks = spread_slots(outs[2])
            attention_total = reduce_attention(outs[1], False, grad_blocks[2])
        results[layer] = (attention_total, expert_totals)

    def columns(layer, start, stop):
        return results[layer][0][:, start:stop]

    deltas = [
        jnp.stack([columns(layer, i * width, (i + 1) * width) for layer in range(LAYERS)])
        for i in range(4)
    ]
    gain_deltas = [
        jnp.stack([columns(layer, 4 * width + i, 4 * width + i + 1)[:, 0] for layer in range(LAYERS)])
        for i in range(2)
    ]
    delta_in = jnp.stack(
        [jnp.stack([piece[:, :units] for piece in results[layer][1]]) for layer in range(LAYERS)]
    )
    delta_out = jnp.stack(
        [jnp.stack([piece[:, units:].T for piece in results[layer][1]]) for layer in range(LAYERS)]
    )
    return (mixed, grad, *deltas, *gain_deltas, delta_in, delta_out)


def solution(mesh):
    placed = (
        P(("dp", "expert"), None),
        P(("dp", "expert"), None),
        P(("dp", "expert")),
        P(("dp", "expert"), None),
        P(None, ("dp", "expert"), None),
        P(None, ("dp", "expert"), None),
        P(None, ("dp", "expert"), None),
        P(None, ("dp", "expert"), None),
        P(None, ("dp", "expert")),
        P(None, ("dp", "expert")),
        P(None, None, "dp", "expert"),
        P(None, None, "expert", "dp"),
        P(("dp", "expert"), None),
    )
    return jax.shard_map(
        on_device,
        mesh=mesh,
        in_specs=placed,
        out_specs=(
            P(("dp", "expert"), None),
            P(("dp", "expert"), None),
            P(None, ("dp", "expert"), None),
            P(None, ("dp", "expert"), None),
            P(None, ("dp", "expert"), None),
            P(None, ("dp", "expert"), None),
            P(None, ("dp", "expert")),
            P(None, ("dp", "expert")),
            P(None, None, "dp", "expert"),
            P(None, None, "expert", "dp"),
        ),
        check_vma=False,
    )
```

```python
from functools import partial

import jax
import jax.numpy as jnp
from jax import lax
from jax.experimental import pallas as pl
from jax.experimental.pallas import tpu as pltpu
from jax.sharding import PartitionSpec as P

HEADS = 12
HEAD_DIM = 64
EXPERTS = 3
LAYERS = 2
MOST = 144

SLOTS = EXPERTS * MOST
PAIR = 2 * HEAD_DIM
epsilon = 1e-05
score_scale = 0.125
FAR = -1e30
RING_MOST = 8
VMEM_BYTES = 56 << 20
f32 = jnp.float32
bf16 = jnp.bfloat16


def mat(left, right):
    return jnp.dot(left, right, preferred_element_type=f32)


def contract_rows(left, right):
    return lax.dot_general(left, right, (((0,), (0,)), ((), ())), preferred_element_type=f32)


def contract_cols(left, right):
    return lax.dot_general(left, right, (((1,), (1,)), ((), ())), preferred_element_type=f32)


def norm_parts(values):
    average = jnp.mean(values, -1, keepdims=True)
    centered = values - average
    spread = jnp.mean(centered * centered, -1, keepdims=True)
    rate = lax.rsqrt(spread + epsilon)
    return centered * rate, rate


def norm_back(unit, rate, scaled_grad):
    first = jnp.mean(scaled_grad, -1, keepdims=True)
    second = jnp.mean(scaled_grad * unit, -1, keepdims=True)
    return rate * (scaled_grad - first - unit * second)


def cost(micros):
    return pl.CostEstimate(
        flops=micros * 10**5, transcendentals=0, bytes_accessed=micros * 10**2
    )


def whole_call(body, out_shape, scratch_shapes=(), name=None, micros=15):
    return pl.pallas_call(
        body,
        out_shape=out_shape,
        scratch_shapes=scratch_shapes,
        compiler_params=pltpu.CompilerParams(vmem_limit_bytes=VMEM_BYTES),
        cost_estimate=cost(micros),
        name=name,
    )


def pack_body(*refs):
    weight_refs, gain_refs, out_refs = refs[:4], refs[4:6], refs[6:]
    rows, width = weight_refs[0].shape[1:]
    lane = lax.broadcasted_iota(jnp.int32, (rows, PAIR), 1)
    diagonal = lax.broadcasted_iota(jnp.int32, (rows, rows), 0) == lax.broadcasted_iota(
        jnp.int32, (rows, rows), 1
    )
    for layer, out_ref in enumerate(out_refs):
        for place, weight_ref in enumerate(weight_refs):
            out_ref[:, place * width : (place + 1) * width] = weight_ref[layer]
        columns = [
            jnp.sum(jnp.where(diagonal, ref[layer : layer + 1, :].astype(f32), 0.0), 1, keepdims=True)
            for ref in gain_refs
        ]
        out_ref[:, 4 * width :] = jnp.where(
            lane == 0, columns[0], jnp.where(lane == 1, columns[1], 0.0)
        ).astype(bf16)


def attend_forward_body(first, *refs):
    if first:
        rows_ref, spot_ref, bias_ref, weight_ref = refs[:4]
        outs = refs[4:]
        rows = rows_ref[...].astype(f32)
    else:
        rows_ref, part_a_ref, part_b_ref, spot_ref, bias_ref, weight_ref = refs[:6]
        outs = refs[6:]
        spot = spot_ref[...]
        rows = rows_ref[...] + mat(spot, part_a_ref[...]) + mat(spot, part_b_ref[...])
    width = rows.shape[1]
    gains = weight_ref[:, 4 * width :].astype(f32).T
    triple_ref, logs_ref, context_ref, hidden_ref, slots_ref = outs[:5]
    if not first:
        outs[5][...] = rows
    unit, _ = norm_parts(rows)
    normed = (unit * gains[0:1, :]).astype(bf16)
    triple_ref[...] = mat(normed, weight_ref[:, : 3 * width]).astype(bf16)
    row_count = rows.shape[0]
    lane = lax.broadcasted_iota(jnp.int32, (row_count, PAIR), 1)
    logs_ref[...] = jnp.zeros_like(logs_ref)

    def one_pair(pair, carry):
        at = pl.multiple_of(pair * PAIR, PAIR)
        query = triple_ref[:, pl.ds(at, PAIR)]
        key = triple_ref[:, pl.ds(at + width, PAIR)]
        value = triple_ref[:, pl.ds(at + 2 * width, PAIR)]
        sides = []
        logs = logs_ref[...]
        for side in range(2):
            mine = (lane >= HEAD_DIM) if side else (lane < HEAD_DIM)
            scores = contract_cols(jnp.where(mine, query, jnp.zeros((), bf16)), key)
            scores = scores * score_scale + bias_ref[...]
            highest = jnp.max(scores, 1, keepdims=True)
            powers = jnp.exp(scores - highest)
            totals = jnp.sum(powers, 1, keepdims=True)
            probs = (powers * (1.0 / totals)).astype(bf16)
            sides.append(mat(probs, value))
            logs = jnp.where(lane == 2 * pair + side, highest + jnp.log(totals), logs)
        logs_ref[...] = logs
        context_ref[:, pl.ds(at, PAIR)] = jnp.where(lane < HEAD_DIM, sides[0], sides[1]).astype(bf16)
        return carry

    lax.fori_loop(0, HEADS // 2, one_pair, 0)
    hidden = rows + mat(context_ref[...], weight_ref[:, 3 * width : 4 * width])
    hidden_ref[...] = hidden
    unit, _ = norm_parts(hidden)
    second = (unit * gains[1:2, :]).astype(bf16)
    slots_ref[...] = contract_rows(spot_ref[...], second).astype(bf16)


def attend_backward_body(last, *refs):
    (
        part_a_ref,
        part_b_ref,
        grad_ref,
        hidden_ref,
        rows_ref,
        triple_ref,
        logs_ref,
        context_ref,
        spot_ref,
        bias_ref,
        weight_ref,
    ) = refs[:11]
    slots_ref = None
    grad_out_ref, weight_grad_ref = refs[11:13]
    if not last:
        slots_ref = refs[13]
    context_grad_ref, triple_grad_ref = refs[-2:]
    width = rows_ref.shape[1]
    gains = weight_ref[:, 4 * width :].astype(f32).T
    spot = spot_ref[...]
    second_grad = mat(spot, part_a_ref[...]) + mat(spot, part_b_ref[...])
    unit, rate = norm_parts(hidden_ref[...])
    second_gain_grad = jnp.sum(second_grad * unit, 0, keepdims=True)
    hidden_grad = grad_ref[...] + norm_back(unit, rate, second_grad * gains[1:2, :])
    row_count, width = hidden_grad.shape
    grad_out_ref[...] = hidden_grad
    branch = hidden_grad.astype(bf16)
    context_grad_ref[...] = contract_cols(branch, weight_ref[:, 3 * width : 4 * width]).astype(bf16)
    output_grad = contract_rows(context_ref[...], branch).astype(bf16)
    weight_grad_ref[:, 3 * width : 4 * width] = output_grad
    lane = lax.broadcasted_iota(jnp.int32, (row_count, PAIR), 1)

    def one_pair(pair, carry):
        at = pl.multiple_of(pair * PAIR, PAIR)
        query = triple_ref[:, pl.ds(at, PAIR)]
        key = triple_ref[:, pl.ds(at + width, PAIR)]
        value = triple_ref[:, pl.ds(at + 2 * width, PAIR)]
        gone = context_grad_ref[:, pl.ds(at, PAIR)]
        zero = jnp.zeros((), bf16)
        query_sides, key_sides, value_sides = [], [], []
        for side in range(2):
            mine = (lane >= HEAD_DIM) if side else (lane < HEAD_DIM)
            log_total = jnp.sum(
                jnp.where(lane == 2 * pair + side, logs_ref[...], 0.0), 1, keepdims=True
            )
            scores = contract_cols(jnp.where(mine, query, zero), key)
            scores = scores * score_scale + bias_ref[...]
            probs = jnp.exp(scores - log_total)
            prob_grad = contract_cols(jnp.where(mine, gone, zero), value)
            inner = jnp.sum(probs * prob_grad, 1, keepdims=True)
            score_grad = (probs * (prob_grad - inner)).astype(bf16)
            query_sides.append(mat(score_grad, key))
            key_sides.append(contract_rows(score_grad, query))
            value_sides.append(contract_rows(probs.astype(bf16), gone))
        left = lane < HEAD_DIM
        triple_grad_ref[:, pl.ds(at, PAIR)] = (
            score_scale * jnp.where(left, query_sides[0], query_sides[1])
        ).astype(bf16)
        triple_grad_ref[:, pl.ds(at + width, PAIR)] = (
            score_scale * jnp.where(left, key_sides[0], key_sides[1])
        ).astype(bf16)
        triple_grad_ref[:, pl.ds(at + 2 * width, PAIR)] = jnp.where(
            left, value_sides[0], value_sides[1]
        ).astype(bf16)
        return carry

    lax.fori_loop(0, HEADS // 2, one_pair, 0)
    unit, rate = norm_parts(rows_ref[...].astype(f32))
    normed = (unit * gains[0:1, :]).astype(bf16)
    triple_grad = triple_grad_ref[...]
    weight_grad_ref[:, : 3 * width] = contract_rows(normed, triple_grad).astype(bf16)
    normed_grad = contract_cols(triple_grad, weight_ref[:, : 3 * width])
    first_gain_grad = jnp.sum(normed_grad * unit, 0, keepdims=True)
    out_grad = grad_out_ref[...] + norm_back(unit, rate, normed_grad * gains[0:1, :])
    grad_out_ref[...] = out_grad
    if slots_ref is not None:
        slots_ref[...] = contract_rows(spot, out_grad.astype(bf16)).astype(bf16)
    which = lax.broadcasted_iota(jnp.int32, (PAIR, width), 0)
    gain_rows = jnp.where(
        which == 0, first_gain_grad, jnp.where(which == 1, second_gain_grad, 0.0)
    )
    weight_grad_ref[:, 4 * width :] = gain_rows.T.astype(bf16)


def expert_forward_body(*refs):
    block_refs, weight_ref = refs[:4], refs[4]
    out_refs, active_ref, slope_ref = refs[5:9], refs[9], refs[10]
    width = block_refs[0].shape[1]
    units = weight_ref.shape[1] // 2
    for half in range(2):
        rows = jnp.concatenate([block_refs[2 * half][...], block_refs[2 * half + 1][...]], 0)
        before = mat(rows, weight_ref[:, :units])
        share = 0.5 + 0.5 * lax.erf(before * 0.7071067811865476)
        slope = share + before * (0.3989422804014327 * jnp.exp(-0.5 * before * before))
        active = (before * share).astype(bf16)
        span = slice(half * 2 * MOST, (half + 1) * 2 * MOST)
        active_ref[span, :] = active
        slope_ref[span, :] = slope.astype(bf16)
        sums = contract_cols(active, weight_ref[:, units:]).astype(bf16)
        out_refs[2 * half][...] = sums[:MOST]
        out_refs[2 * half + 1][...] = sums[MOST:]


def expert_backward_body(split, *refs):
    place_ref, *refs = refs
    grad_refs, block_refs = refs[:4], refs[4:8]
    active_ref, slope_ref, weight_ref = refs[8:11]
    out_refs, total_refs = refs[11:15], refs[15:]
    units = weight_ref.shape[1] // 2
    grads = jnp.concatenate([ref[...] for ref in grad_refs], 0)
    rows = jnp.concatenate([ref[...] for ref in block_refs], 0)
    active_grad = mat(grads, weight_ref[:, units:])
    before_grad = (active_grad * slope_ref[...].astype(f32)).astype(bf16)
    sums = contract_cols(before_grad, weight_ref[:, :units]).astype(bf16)
    for place in range(4):
        out_refs[place][...] = sums[place * MOST : (place + 1) * MOST]
    step = pl.program_id(0)
    for left, right, start in ((rows, before_grad, 0), (grads, active_ref[...], units)):
        grad = contract_rows(left, right).astype(bf16)
        span = slice(start, start + units)
        if not split:
            total_refs[0][:, span] = grad
            continue
        ring, mine = place_ref[0], place_ref[1]
        outer, count = total_refs[0].shape[:2]

        def piece(block, half):
            first = (2 * block + half) * count
            return grad[first : first + count]

        for expert in range(EXPERTS):
            for half in range(2):

                @pl.when((step == expert) & (mine == half))
                def _():
                    for block in range(outer):
                        at = lax.rem(block - ring + outer, outer)
                        kept_ref, sent_ref = total_refs[2 * expert : 2 * expert + 2]
                        kept_ref[at, :, span] = piece(block, half)
                        sent_ref[at, :, span] = piece(block, 1 - half)


def finish_body(places, *refs):
    outs = refs[-8:]
    at = 0
    units = outs[6].shape[3]
    for layer, experts in enumerate(places):
        for expert, (source, start) in enumerate(experts):
            values = refs[at + source]
            outs[6][layer, expert] = values[:, start : start + units].astype(f32)
            outs[7][layer, expert] = values[:, start + units : start + 2 * units].astype(f32)
        at += max(source for source, _ in experts) + 1
        sums = refs[at][...].astype(f32)
        at += 1
        rows, width = outs[0].shape[1:]
        for place in range(4):
            outs[place][layer] = sums[:, place * width : (place + 1) * width]
        diagonal = lax.broadcasted_iota(jnp.int32, (rows, rows), 0) == lax.broadcasted_iota(
            jnp.int32, (rows, rows), 1
        )
        for place in range(2):
            column = sums[:, 4 * width + place : 4 * width + place + 1]
            outs[4 + place][layer : layer + 1, :] = jnp.sum(
                jnp.where(diagonal, column, 0.0), 0, keepdims=True
            )


def expert_forward(blocks, weights):
    width = blocks[0].shape[1]
    units = weights.shape[1] // (2 * EXPERTS)
    block = pl.BlockSpec((MOST, width), lambda e: (e, 0))
    kept = pl.BlockSpec((4 * MOST, units), lambda e: (e, 0))
    outs = pl.pallas_call(
        expert_forward_body,
        grid=(EXPERTS,),
        in_specs=[block] * 4 + [pl.BlockSpec((width, 2 * units), lambda e: (0, e))],
        out_specs=[block] * 4 + [kept] * 2,
        out_shape=[jax.ShapeDtypeStruct((SLOTS, width), bf16)] * 4
        + [jax.ShapeDtypeStruct((4 * SLOTS, units), bf16)] * 2,
        compiler_params=pltpu.CompilerParams(vmem_limit_bytes=VMEM_BYTES),
        cost_estimate=cost(10),
        name="expert_forward",
    )(*blocks, weights)
    return outs[:4], outs[4], outs[5]


def expert_backward(grads, blocks, active, slope, weights, split):
    width = blocks[0].shape[1]
    units = weights.shape[1] // (2 * EXPERTS)
    count, me = lax.axis_size("dp"), lax.axis_index("dp")
    block = pl.BlockSpec((MOST, width), lambda e, *_: (e, 0))
    kept = pl.BlockSpec((4 * MOST, units), lambda e, *_: (e, 0))
    square = pl.BlockSpec((width, 2 * units), lambda e, *_: (0, e))
    out_specs = [block] * 4
    out_shape = [jax.ShapeDtypeStruct((SLOTS, width), bf16)] * 4
    if split:
        pair = (count // 2, width // count, 2 * units)
        out_specs += [pl.BlockSpec(pair, lambda e, *_: (0, 0, 0))] * (2 * EXPERTS)
        out_shape += [jax.ShapeDtypeStruct(pair, bf16)] * (2 * EXPERTS)
    else:
        out_specs += [square]
        out_shape += [jax.ShapeDtypeStruct(weights.shape, bf16)]
    outs = pl.pallas_call(
        partial(expert_backward_body, split),
        grid_spec=pltpu.PrefetchScalarGridSpec(
            num_scalar_prefetch=1,
            grid=(EXPERTS,),
            in_specs=[block] * 8 + [kept] * 2 + [square],
            out_specs=out_specs,
        ),
        out_shape=out_shape,
        compiler_params=pltpu.CompilerParams(vmem_limit_bytes=VMEM_BYTES),
        cost_estimate=cost(16),
        name="expert_backward",
    )(
        jnp.stack([me // 2, lax.rem(me, 2)]).astype(jnp.int32),
        *grads,
        *blocks,
        active,
        slope,
        weights,
    )
    return outs[:4], outs[4:]


def swap(values, flip):
    count = lax.axis_size("expert")
    return lax.ppermute(values, "expert", [(i, i ^ flip) for i in range(count)])


def spread_slots(slots):
    across = swap(slots, 2)
    beside = swap(slots, 1)
    corner = swap(across, 1)
    return [slots, beside, across, corner]


def collect_core(parts):
    own, beside, across, corner = parts
    corner_in = swap(corner, 1)
    beside_in = swap(beside, 1)
    far = (across.astype(f32) + corner_in.astype(f32)).astype(bf16)
    near = (own.astype(f32) + beside_in.astype(f32)).astype(bf16)
    return near, far


def collect_slots(parts):
    near, far = collect_core(parts)
    return near, swap(far, 2)


def pair_perm(count):
    return [(i, i ^ 1) for i in range(count)]


def ring_perm(count):
    return [(i, (i + 2) % count) for i in range(count)]


def gather_rows(shard, events):
    count = lax.axis_size("dp")
    if count > RING_MOST:
        return lax.all_gather(shard, "dp", axis=0, tiled=True)
    line_done, pair_done, all_done = events
    me = lax.axis_index("dp")
    rows, cols = shard.shape
    full = jnp.zeros((count * rows, cols), shard.dtype)
    moving, _ = tie(shard, line_done)
    for step in range(count // 2):
        source = lax.rem(me - 2 * step + count, count)
        mate = moving
        if step == 0:
            mate, _ = tie(mate, pair_done)
        mate = lax.ppermute(mate, "dp", pair_perm(count))
        mate, _ = tie(mate, all_done)
        full = lax.dynamic_update_slice(full, moving, (source * rows, 0))
        full = lax.dynamic_update_slice(full, mate, ((source ^ 1) * rows, 0))
        if step + 1 < count // 2:
            moving = lax.ppermute(moving, "dp", ring_perm(count))
            if step > 0:
                moving, _ = tie(moving, all_done)
    return full


def tie(*values):
    return lax.optimization_barrier(values)


def add(left, right):
    return left.astype(f32) + right.astype(f32)


def pick(values, at, axis):
    return lax.dynamic_index_in_dim(values, at, axis, keepdims=False)


def put(values, piece, at, axis):
    return lax.dynamic_update_index_in_dim(values, piece, at, axis)


def shift_perm(count, step):
    return [(i, (i + 2 * step) % count) for i in range(count)]


def gather_attention(shard):
    count = lax.axis_size("dp")
    if count > RING_MOST:
        return lax.all_gather(shard, ("dp", "expert"), axis=0, tiled=True), (shard,) * 3
    rows, cols = shard.shape
    outer = count // 2
    me = lax.axis_index("dp")
    line = me // 2
    quad = put(jnp.zeros((outer, rows, cols), shard.dtype), shard, line, 0)
    for step in range(1, outer):
        got = lax.ppermute(shard, "dp", shift_perm(count, step))
        quad = put(quad, got, lax.rem(line - step + outer, outer), 0)
    mate = lax.ppermute(quad, "dp", pair_perm(count))
    both = jnp.zeros((outer, 2, rows, cols), shard.dtype)
    both = put(put(both, quad, lax.rem(me, 2), 1), mate, 1 - lax.rem(me, 2), 1)
    across = swap(both, 2)
    full, corner = join_sides(both, across)
    return full, (got, mate, corner)


def join_sides(both, across):
    outer, _, rows, cols = both.shape
    sides, side = lax.axis_size("expert"), lax.axis_index("expert")
    full = jnp.zeros((outer, 2, sides, rows, cols), both.dtype)
    corner = swap(across, 1)
    full = put(full, both, side, 2)
    full = put(full, swap(both, 1), side ^ 1, 2)
    full = put(full, across, side ^ 2, 2)
    full = put(full, corner, side ^ 3, 2)
    return full.reshape(-1, cols), corner


def swap_pair(values):
    return lax.ppermute(values, "dp", pair_perm(lax.axis_size("dp")))


def ring_step(values):
    return lax.ppermute(values, "dp", ring_perm(lax.axis_size("dp")))


def ring_total(blocks):
    moving = blocks(lax.axis_size("dp") // 2 - 1)
    for step in reversed(range(lax.axis_size("dp") // 2 - 1)):
        moving = add(ring_step(moving), blocks(step))
        if step:
            moving = moving.astype(bf16)
    return moving


def halve_core(blocks, axis):
    core = lax.rem(lax.axis_index("expert"), 2)
    got = swap(pick(blocks, 1 - core, axis), 1)
    return add(pick(blocks, core, axis), got).astype(bf16)


def halve_line(blocks, axis):
    line = lax.axis_index("expert") // 2
    got = swap(pick(blocks, 1 - line, axis), 2)
    return add(pick(blocks, line, axis), got).astype(bf16)


def halve_pair(blocks, axis):
    mine = lax.rem(lax.axis_index("dp"), 2)
    got = lax.ppermute(pick(blocks, 1 - mine, axis), "dp", pair_perm(lax.axis_size("dp")))
    return add(pick(blocks, mine, axis), got).astype(bf16)


def reduce_line(blocks):
    count = lax.axis_size("dp")
    outer = count // 2
    line = lax.axis_index("dp") // 2
    total = pick(blocks, line, 0).astype(f32)
    for step in range(1, outer):
        sent = pick(blocks, lax.rem(line + step, outer), 0)
        total = total + lax.ppermute(sent, "dp", shift_perm(count, step)).astype(f32)
    return total


def attention_blocks(values):
    return values.reshape(lax.axis_size("dp") // 2, 2, lax.axis_size("expert") // 2, 2, -1, values.shape[1])


def reduce_everywhere(values):
    return lax.psum_scatter(values, ("dp", "expert"), scatter_dimension=0, tiled=True).astype(f32)


def on_device(
    tokens,
    groups,
    key_mask,
    routes,
    query_weight,
    key_weight,
    value_weight,
    output_weight,
    norm_first,
    norm_second,
    expert_in,
    expert_out,
    cotangent,
):
    both = ("dp", "expert")
    row_count, width = tokens.shape
    units = expert_in.shape[3]
    shard_rows = expert_in.shape[2]
    own_rows = query_weight.shape[1]

    attention_shards = whole_call(
        pack_body,
        [jax.ShapeDtypeStruct((own_rows, 4 * width + PAIR), bf16)] * LAYERS,
        name="pack_attention",
    )(query_weight, key_weight, value_weight, output_weight, norm_first, norm_second)

    def expert_shard(layer):
        pieces = jnp.concatenate(
            [expert_in[layer], jnp.transpose(expert_out[layer], (0, 2, 1))], 2
        )
        return jnp.transpose(pieces, (1, 0, 2)).reshape(shard_rows, EXPERTS * 2 * units)

    count = lax.axis_size("dp")
    small = count <= RING_MOST
    attention_first, events = gather_attention(attention_shards[0])
    attention_all = [
        attention_first,
        lax.all_gather(attention_shards[1], both, axis=0, tiled=True),
    ]
    experts_all = [
        gather_rows(expert_shard(0), events),
        lax.all_gather(expert_shard(1), "dp", axis=0, tiled=True),
    ]

    route = routes[:, 0]
    place = jnp.arange(row_count, dtype=jnp.int32)
    earlier = (route[:, None] == route[None, :]) & (place[None, :] < place[:, None])
    slot_of = route * MOST + jnp.sum(earlier.astype(jnp.int32), 1)
    spot = (slot_of[:, None] == jnp.arange(SLOTS, dtype=jnp.int32)[None, :]).astype(bf16)
    group = groups[0]
    allowed = (group[:, None] == group[None, :]) & (
        (key_mask[None, :] == 1) | (place[:, None] == place[None, :])
    )
    bias = jnp.where(allowed, 0.0, FAR).astype(f32)

    last_slots = contract_rows(spot, cotangent.astype(bf16)).astype(bf16)
    last_slots, _ = tie(last_slots, events[2])
    last_grads = spread_slots(last_slots)

    def shape_of(rows, cols, kind):
        return jax.ShapeDtypeStruct((rows, cols), kind)

    saved = []
    rows = tokens
    parts = None
    for layer in range(LAYERS):
        first = layer == 0
        weight = attention_all[layer]
        outs = whole_call(
            partial(attend_forward_body, first),
            [
                shape_of(row_count, 3 * width, bf16),
                shape_of(row_count, PAIR, f32),
                shape_of(row_count, width, bf16),
                shape_of(row_count, width, f32),
                shape_of(SLOTS, width, bf16),
            ]
            + ([] if first else [shape_of(row_count, width, f32)]),
            name="attend_forward",
        )(*([rows] if first else [rows, *parts]), spot, bias, weight)
        triple, logs, context, hidden, slots = outs[:5]
        inputs = tokens if first else outs[5]
        if first:
            slots, _ = tie(slots, last_grads[2])
        blocks = spread_slots(slots)
        sums, active, slope = expert_forward(blocks, experts_all[layer])
        if layer + 1 < LAYERS:
            parts = collect_slots(sums)
        rows = hidden
        saved.append((inputs, triple, logs, context, hidden, blocks, active, slope, weight))
    final_near, final_far = collect_core(sums)

    def expert_part(layer, grads, split):
        blocks, active, slope = saved[layer][5:8]
        return expert_backward(grads, blocks, active, slope, experts_all[layer], split)

    def attend_part(layer, parts, grad):
        inputs, triple, logs, context, hidden = saved[layer][:5]
        weight = saved[layer][8]
        last = layer == 0
        return whole_call(
            partial(attend_backward_body, last),
            [shape_of(row_count, width, f32), shape_of(width, 4 * width + PAIR, bf16)]
            + ([] if last else [shape_of(SLOTS, width, bf16)]),
            scratch_shapes=[
                pltpu.VMEM((row_count, width), bf16),
                pltpu.VMEM((row_count, 3 * width), bf16),
            ],
            name="attend_backward",
        )(*parts, grad, hidden, inputs, triple, logs, context, spot, bias, weight)

    def offload(values):
        return lax.psum_scatter(values, "dp", scatter_dimension=0, tiled=True)

    together = tuple((0, 2 * units * expert) for expert in range(EXPERTS))
    if small:
        sums, (whole,) = expert_part(1, last_grads, False)
        second_experts = offload(whole)
        parts = collect_slots(sums)
        outs = attend_part(1, parts, cotangent)
        held = halve_core(attention_blocks(outs[1]), 3)
        grad_blocks = spread_slots(outs[2])
        *grad_blocks, held = tie(*grad_blocks, held)
        held = halve_line(held, 2)
        sums, pairs = expert_part(0, grad_blocks, True)
        *sums, held = tie(*sums, held)
        kepts = list(pairs[::2])
        gots = [swap_pair(sent) for sent in pairs[1::2]]
        parts = collect_slots(sums)
        outs = attend_part(0, parts, outs[0])
        whole, held, gots[0], gots[1], second_experts = tie(
            outs[1], held, gots[0], gots[1], second_experts
        )
        second_total = reduce_line(halve_pair(held, 1))

        def block(expert, step):
            return add(kepts[expert][step], gots[expert][step]).astype(bf16)

        def onward(expert, moving, step):
            return add(moving, block(expert, step)).astype(bf16)

        blocks = halve_core(attention_blocks(whole), 3)
        blocks, kepts[0] = tie(blocks, kepts[0])
        blocks = halve_line(blocks, 2)
        one = ring_step(block(0, 3))
        one, kepts[1] = tie(one, kepts[1])
        one = ring_step(onward(0, one, 2))
        two = ring_step(block(1, 3))
        two, kepts[2], final_far = tie(two, kepts[2], final_far)
        final_far = swap(final_far, 2)
        first_total = reduce_line(halve_pair(blocks, 1))
        one = add(ring_step(onward(0, one, 1)), block(0, 0))
        two = ring_step(onward(1, two, 2))
        two = add(ring_step(onward(1, two, 1)), block(1, 0))
        three = ring_step(block(2, 3))
        three = ring_step(onward(2, three, 2))
        three = add(ring_step(onward(2, three, 1)), block(2, 0))
        first_experts = [one, two, three]
        places = (tuple((expert, 0) for expert in range(EXPERTS)), together)
    else:
        sums, (whole,) = expert_part(1, last_grads, False)
        second_experts = offload(whole)
        outs = attend_part(1, collect_slots(sums), cotangent)
        second_total = reduce_everywhere(outs[1])
        sums, (whole,) = expert_part(0, spread_slots(outs[2]), False)
        first_experts = [offload(whole)]
        outs = attend_part(0, collect_slots(sums), outs[0])
        first_total = reduce_everywhere(outs[1])
        final_far = swap(final_far, 2)
        places = (together, together)
    mixed = (rows + mat(spot, final_near) + mat(spot, final_far)).astype(bf16)
    square = jax.ShapeDtypeStruct((LAYERS, own_rows, width), f32)
    line = jax.ShapeDtypeStruct((LAYERS, own_rows), f32)
    wide = jax.ShapeDtypeStruct((LAYERS, EXPERTS, shard_rows, units), f32)
    deltas = whole_call(
        partial(finish_body, places), [square] * 4 + [line] * 2 + [wide] * 2, name="finish"
    )(*first_experts, first_total, second_experts, second_total)
    return (mixed, outs[0], *deltas[:7], jnp.swapaxes(deltas[7], 2, 3))


def solution(mesh):
    placed = (
        P(("dp", "expert"), None),
        P(("dp", "expert"), None),
        P(("dp", "expert")),
        P(("dp", "expert"), None),
        P(None, ("dp", "expert"), None),
        P(None, ("dp", "expert"), None),
        P(None, ("dp", "expert"), None),
        P(None, ("dp", "expert"), None),
        P(None, ("dp", "expert")),
        P(None, ("dp", "expert")),
        P(None, None, "dp", "expert"),
        P(None, None, "expert", "dp"),
        P(("dp", "expert"), None),
    )
    return jax.shard_map(
        on_device,
        mesh=mesh,
        in_specs=placed,
        out_specs=(
            P(("dp", "expert"), None),
            P(("dp", "expert"), None),
            P(None, ("dp", "expert"), None),
            P(None, ("dp", "expert"), None),
            P(None, ("dp", "expert"), None),
            P(None, ("dp", "expert"), None),
            P(None, ("dp", "expert")),
            P(None, ("dp", "expert")),
            P(None, None, "dp", "expert"),
            P(None, None, "expert", "dp"),
        ),
        check_vma=False,
    )
```

```python
from functools import partial

import jax
import jax.numpy as jnp
from jax import lax
from jax.experimental import pallas as pl
from jax.experimental.pallas import tpu as pltpu
from jax.sharding import PartitionSpec as P

HEADS = 12
HEAD_DIM = 64
EXPERTS = 3
LAYERS = 2
MOST = 144

SLOTS = EXPERTS * MOST
PAIR = 2 * HEAD_DIM
epsilon = 1e-05
score_scale = 0.125
FAR = -1e30
RING_MOST = 8
VMEM_BYTES = 56 << 20
f32 = jnp.float32
bf16 = jnp.bfloat16


def mat(left, right):
    return jnp.dot(left, right, preferred_element_type=f32)


def contract_rows(left, right):
    return lax.dot_general(left, right, (((0,), (0,)), ((), ())), preferred_element_type=f32)


def contract_cols(left, right):
    return lax.dot_general(left, right, (((1,), (1,)), ((), ())), preferred_element_type=f32)


def norm_parts(values):
    average = jnp.mean(values, -1, keepdims=True)
    centered = values - average
    spread = jnp.mean(centered * centered, -1, keepdims=True)
    rate = lax.rsqrt(spread + epsilon)
    return centered * rate, rate


def norm_back(unit, rate, scaled_grad):
    first = jnp.mean(scaled_grad, -1, keepdims=True)
    second = jnp.mean(scaled_grad * unit, -1, keepdims=True)
    return rate * (scaled_grad - first - unit * second)


def cost(micros):
    return pl.CostEstimate(
        flops=micros * 10**5, transcendentals=0, bytes_accessed=micros * 10**2
    )


def whole_call(body, out_shape, scratch_shapes=(), name=None, micros=15):
    return pl.pallas_call(
        body,
        out_shape=out_shape,
        scratch_shapes=scratch_shapes,
        compiler_params=pltpu.CompilerParams(vmem_limit_bytes=VMEM_BYTES),
        cost_estimate=cost(micros),
        name=name,
    )


def pack_body(*refs):
    weight_refs, gain_refs, out_refs = refs[:4], refs[4:6], refs[6:]
    rows, width = weight_refs[0].shape[1:]
    lane = lax.broadcasted_iota(jnp.int32, (rows, PAIR), 1)
    diagonal = lax.broadcasted_iota(jnp.int32, (rows, rows), 0) == lax.broadcasted_iota(
        jnp.int32, (rows, rows), 1
    )
    for layer, out_ref in enumerate(out_refs):
        for place, weight_ref in enumerate(weight_refs):
            out_ref[:, place * width : (place + 1) * width] = weight_ref[layer]
        columns = [
            jnp.sum(jnp.where(diagonal, ref[layer : layer + 1, :].astype(f32), 0.0), 1, keepdims=True)
            for ref in gain_refs
        ]
        out_ref[:, 4 * width :] = jnp.where(
            lane == 0, columns[0], jnp.where(lane == 1, columns[1], 0.0)
        ).astype(bf16)


def attend_forward_body(first, *refs):
    if first:
        rows_ref, spot_ref, bias_ref, weight_ref = refs[:4]
        outs = refs[4:]
        rows = rows_ref[...].astype(f32)
    else:
        rows_ref, part_a_ref, part_b_ref, spot_ref, bias_ref, weight_ref = refs[:6]
        outs = refs[6:]
        spot = spot_ref[...]
        rows = rows_ref[...] + mat(spot, part_a_ref[...]) + mat(spot, part_b_ref[...])
    width = rows.shape[1]
    gains = weight_ref[:, 4 * width :].astype(f32).T
    triple_ref, logs_ref, context_ref, hidden_ref, slots_ref = outs[:5]
    if not first:
        outs[5][...] = rows
    unit, _ = norm_parts(rows)
    normed = (unit * gains[0:1, :]).astype(bf16)
    triple_ref[...] = mat(normed, weight_ref[:, : 3 * width]).astype(bf16)
    row_count = rows.shape[0]
    lane = lax.broadcasted_iota(jnp.int32, (row_count, PAIR), 1)
    logs_ref[...] = jnp.zeros_like(logs_ref)

    def one_pair(pair, carry):
        at = pl.multiple_of(pair * PAIR, PAIR)
        query = triple_ref[:, pl.ds(at, PAIR)]
        key = triple_ref[:, pl.ds(at + width, PAIR)]
        value = triple_ref[:, pl.ds(at + 2 * width, PAIR)]
        sides = []
        logs = logs_ref[...]
        for side in range(2):
            mine = (lane >= HEAD_DIM) if side else (lane < HEAD_DIM)
            scores = contract_cols(jnp.where(mine, query, jnp.zeros((), bf16)), key)
            scores = scores * score_scale + bias_ref[...]
            highest = jnp.max(scores, 1, keepdims=True)
            powers = jnp.exp(scores - highest)
            totals = jnp.sum(powers, 1, keepdims=True)
            probs = (powers * (1.0 / totals)).astype(bf16)
            sides.append(mat(probs, value))
            logs = jnp.where(lane == 2 * pair + side, highest + jnp.log(totals), logs)
        logs_ref[...] = logs
        context_ref[:, pl.ds(at, PAIR)] = jnp.where(lane < HEAD_DIM, sides[0], sides[1]).astype(bf16)
        return carry

    lax.fori_loop(0, HEADS // 2, one_pair, 0)
    hidden = rows + mat(context_ref[...], weight_ref[:, 3 * width : 4 * width])
    hidden_ref[...] = hidden
    unit, _ = norm_parts(hidden)
    second = (unit * gains[1:2, :]).astype(bf16)
    slots_ref[...] = contract_rows(spot_ref[...], second).astype(bf16)


def attend_backward_body(last, *refs):
    (
        part_a_ref,
        part_b_ref,
        grad_ref,
        hidden_ref,
        rows_ref,
        triple_ref,
        logs_ref,
        context_ref,
        spot_ref,
        bias_ref,
        weight_ref,
    ) = refs[:11]
    slots_ref = None
    grad_out_ref, weight_grad_ref = refs[11:13]
    if not last:
        slots_ref = refs[13]
    context_grad_ref, triple_grad_ref = refs[-2:]
    width = rows_ref.shape[1]
    gains = weight_ref[:, 4 * width :].astype(f32).T
    spot = spot_ref[...]
    second_grad = mat(spot, part_a_ref[...]) + mat(spot, part_b_ref[...])
    unit, rate = norm_parts(hidden_ref[...])
    second_gain_grad = jnp.sum(second_grad * unit, 0, keepdims=True)
    hidden_grad = grad_ref[...] + norm_back(unit, rate, second_grad * gains[1:2, :])
    row_count, width = hidden_grad.shape
    grad_out_ref[...] = hidden_grad
    branch = hidden_grad.astype(bf16)
    context_grad_ref[...] = contract_cols(branch, weight_ref[:, 3 * width : 4 * width]).astype(bf16)
    output_grad = contract_rows(context_ref[...], branch).astype(bf16)
    weight_grad_ref[:, 3 * width : 4 * width] = output_grad
    lane = lax.broadcasted_iota(jnp.int32, (row_count, PAIR), 1)

    def one_pair(pair, carry):
        at = pl.multiple_of(pair * PAIR, PAIR)
        query = triple_ref[:, pl.ds(at, PAIR)]
        key = triple_ref[:, pl.ds(at + width, PAIR)]
        value = triple_ref[:, pl.ds(at + 2 * width, PAIR)]
        gone = context_grad_ref[:, pl.ds(at, PAIR)]
        zero = jnp.zeros((), bf16)
        query_sides, key_sides, value_sides = [], [], []
        for side in range(2):
            mine = (lane >= HEAD_DIM) if side else (lane < HEAD_DIM)
            log_total = jnp.sum(
                jnp.where(lane == 2 * pair + side, logs_ref[...], 0.0), 1, keepdims=True
            )
            scores = contract_cols(jnp.where(mine, query, zero), key)
            scores = scores * score_scale + bias_ref[...]
            probs = jnp.exp(scores - log_total)
            prob_grad = contract_cols(jnp.where(mine, gone, zero), value)
            inner = jnp.sum(probs * prob_grad, 1, keepdims=True)
            score_grad = (probs * (prob_grad - inner)).astype(bf16)
            query_sides.append(mat(score_grad, key))
            key_sides.append(contract_rows(score_grad, query))
            value_sides.append(contract_rows(probs.astype(bf16), gone))
        left = lane < HEAD_DIM
        triple_grad_ref[:, pl.ds(at, PAIR)] = (
            score_scale * jnp.where(left, query_sides[0], query_sides[1])
        ).astype(bf16)
        triple_grad_ref[:, pl.ds(at + width, PAIR)] = (
            score_scale * jnp.where(left, key_sides[0], key_sides[1])
        ).astype(bf16)
        triple_grad_ref[:, pl.ds(at + 2 * width, PAIR)] = jnp.where(
            left, value_sides[0], value_sides[1]
        ).astype(bf16)
        return carry

    lax.fori_loop(0, HEADS // 2, one_pair, 0)
    unit, rate = norm_parts(rows_ref[...].astype(f32))
    normed = (unit * gains[0:1, :]).astype(bf16)
    triple_grad = triple_grad_ref[...]
    weight_grad_ref[:, : 3 * width] = contract_rows(normed, triple_grad).astype(bf16)
    normed_grad = contract_cols(triple_grad, weight_ref[:, : 3 * width])
    first_gain_grad = jnp.sum(normed_grad * unit, 0, keepdims=True)
    out_grad = grad_out_ref[...] + norm_back(unit, rate, normed_grad * gains[0:1, :])
    grad_out_ref[...] = out_grad
    if slots_ref is not None:
        slots_ref[...] = contract_rows(spot, out_grad.astype(bf16)).astype(bf16)
    which = lax.broadcasted_iota(jnp.int32, (PAIR, width), 0)
    gain_rows = jnp.where(
        which == 0, first_gain_grad, jnp.where(which == 1, second_gain_grad, 0.0)
    )
    weight_grad_ref[:, 4 * width :] = gain_rows.T.astype(bf16)


def expert_forward_body(*refs):
    block_refs, weight_ref = refs[:4], refs[4]
    out_refs, active_ref, slope_ref = refs[5:9], refs[9], refs[10]
    width = block_refs[0].shape[1]
    units = weight_ref.shape[1] // 2
    for half in range(2):
        rows = jnp.concatenate([block_refs[2 * half][...], block_refs[2 * half + 1][...]], 0)
        before = mat(rows, weight_ref[:, :units])
        share = 0.5 + 0.5 * lax.erf(before * 0.7071067811865476)
        slope = share + before * (0.3989422804014327 * jnp.exp(-0.5 * before * before))
        active = (before * share).astype(bf16)
        span = slice(half * 2 * MOST, (half + 1) * 2 * MOST)
        active_ref[span, :] = active
        slope_ref[span, :] = slope.astype(bf16)
        sums = contract_cols(active, weight_ref[:, units:]).astype(bf16)
        out_refs[2 * half][...] = sums[:MOST]
        out_refs[2 * half + 1][...] = sums[MOST:]


def expert_backward_body(split, *refs):
    place_ref, *refs = refs
    grad_refs, block_refs = refs[:4], refs[4:8]
    active_ref, slope_ref, weight_ref = refs[8:11]
    out_refs, total_refs = refs[11:15], refs[15:]
    units = weight_ref.shape[1] // 2
    grads = jnp.concatenate([ref[...] for ref in grad_refs], 0)
    rows = jnp.concatenate([ref[...] for ref in block_refs], 0)
    active_grad = mat(grads, weight_ref[:, units:])
    before_grad = (active_grad * slope_ref[...].astype(f32)).astype(bf16)
    sums = contract_cols(before_grad, weight_ref[:, :units]).astype(bf16)
    for place in range(4):
        out_refs[place][...] = sums[place * MOST : (place + 1) * MOST]
    step = pl.program_id(0)
    for left, right, start in ((rows, before_grad, 0), (grads, active_ref[...], units)):
        grad = contract_rows(left, right).astype(bf16)
        span = slice(start, start + units)
        if not split:
            total_refs[0][:, span] = grad
            continue
        ring, mine = place_ref[0], place_ref[1]
        outer, count = total_refs[0].shape[:2]

        def piece(block, half):
            first = (2 * block + half) * count
            return grad[first : first + count]

        for expert in range(EXPERTS):
            for half in range(2):

                @pl.when((step == expert) & (mine == half))
                def _():
                    for block in range(outer):
                        at = lax.rem(block - ring + outer, outer)
                        kept_ref, sent_ref = total_refs[2 * expert : 2 * expert + 2]
                        kept_ref[at, :, span] = piece(block, half)
                        sent_ref[at, :, span] = piece(block, 1 - half)


def finish_body(places, *refs):
    outs = refs[-8:]
    at = 0
    units = outs[6].shape[3]
    for layer, experts in enumerate(places):
        for expert, (source, start) in enumerate(experts):
            values = refs[at + source]
            outs[6][layer, expert] = values[:, start : start + units].astype(f32)
            outs[7][layer, expert] = values[:, start + units : start + 2 * units].astype(f32)
        at += max(source for source, _ in experts) + 1
        sums = refs[at][...].astype(f32)
        at += 1
        rows, width = outs[0].shape[1:]
        for place in range(4):
            outs[place][layer] = sums[:, place * width : (place + 1) * width]
        diagonal = lax.broadcasted_iota(jnp.int32, (rows, rows), 0) == lax.broadcasted_iota(
            jnp.int32, (rows, rows), 1
        )
        for place in range(2):
            column = sums[:, 4 * width + place : 4 * width + place + 1]
            outs[4 + place][layer : layer + 1, :] = jnp.sum(
                jnp.where(diagonal, column, 0.0), 0, keepdims=True
            )


def expert_forward(blocks, weights):
    width = blocks[0].shape[1]
    units = weights.shape[1] // (2 * EXPERTS)
    block = pl.BlockSpec((MOST, width), lambda e: (e, 0))
    kept = pl.BlockSpec((4 * MOST, units), lambda e: (e, 0))
    outs = pl.pallas_call(
        expert_forward_body,
        grid=(EXPERTS,),
        in_specs=[block] * 4 + [pl.BlockSpec((width, 2 * units), lambda e: (0, e))],
        out_specs=[block] * 4 + [kept] * 2,
        out_shape=[jax.ShapeDtypeStruct((SLOTS, width), bf16)] * 4
        + [jax.ShapeDtypeStruct((4 * SLOTS, units), bf16)] * 2,
        compiler_params=pltpu.CompilerParams(vmem_limit_bytes=VMEM_BYTES),
        cost_estimate=cost(10),
        name="expert_forward",
    )(*blocks, weights)
    return outs[:4], outs[4], outs[5]


def expert_backward(grads, blocks, active, slope, weights, split):
    width = blocks[0].shape[1]
    units = weights.shape[1] // (2 * EXPERTS)
    count, me = lax.axis_size("dp"), lax.axis_index("dp")
    block = pl.BlockSpec((MOST, width), lambda e, *_: (e, 0))
    kept = pl.BlockSpec((4 * MOST, units), lambda e, *_: (e, 0))
    square = pl.BlockSpec((width, 2 * units), lambda e, *_: (0, e))
    out_specs = [block] * 4
    out_shape = [jax.ShapeDtypeStruct((SLOTS, width), bf16)] * 4
    if split:
        pair = (count // 2, width // count, 2 * units)
        out_specs += [pl.BlockSpec(pair, lambda e, *_: (0, 0, 0))] * (2 * EXPERTS)
        out_shape += [jax.ShapeDtypeStruct(pair, bf16)] * (2 * EXPERTS)
    else:
        out_specs += [square]
        out_shape += [jax.ShapeDtypeStruct(weights.shape, bf16)]
    outs = pl.pallas_call(
        partial(expert_backward_body, split),
        grid_spec=pltpu.PrefetchScalarGridSpec(
            num_scalar_prefetch=1,
            grid=(EXPERTS,),
            in_specs=[block] * 8 + [kept] * 2 + [square],
            out_specs=out_specs,
        ),
        out_shape=out_shape,
        compiler_params=pltpu.CompilerParams(vmem_limit_bytes=VMEM_BYTES),
        cost_estimate=cost(16),
        name="expert_backward",
    )(
        jnp.stack([me // 2, lax.rem(me, 2)]).astype(jnp.int32),
        *grads,
        *blocks,
        active,
        slope,
        weights,
    )
    return outs[:4], outs[4:]


def swap(values, flip):
    count = lax.axis_size("expert")
    return lax.ppermute(values, "expert", [(i, i ^ flip) for i in range(count)])


def spread_slots(slots):
    across = swap(slots, 2)
    beside = swap(slots, 1)
    corner = swap(across, 1)
    return [slots, beside, across, corner]


def collect_core(parts):
    own, beside, across, corner = parts
    corner_in = swap(corner, 1)
    beside_in = swap(beside, 1)
    far = (across.astype(f32) + corner_in.astype(f32)).astype(bf16)
    near = (own.astype(f32) + beside_in.astype(f32)).astype(bf16)
    return near, far


def collect_slots(parts):
    near, far = collect_core(parts)
    return near, swap(far, 2)


def pair_perm(count):
    return [(i, i ^ 1) for i in range(count)]


def ring_perm(count):
    return [(i, (i + 2) % count) for i in range(count)]


def gather_rows(shard, events):
    count = lax.axis_size("dp")
    if count > RING_MOST:
        return lax.all_gather(shard, "dp", axis=0, tiled=True)
    line_done, pair_done, all_done = events
    me = lax.axis_index("dp")
    rows, cols = shard.shape
    full = jnp.zeros((count * rows, cols), shard.dtype)
    moving, _ = tie(shard, line_done)
    for step in range(count // 2):
        source = lax.rem(me - 2 * step + count, count)
        mate = moving
        if step == 0:
            mate, _ = tie(mate, pair_done)
        mate = lax.ppermute(mate, "dp", pair_perm(count))
        mate, _ = tie(mate, all_done)
        full = lax.dynamic_update_slice(full, moving, (source * rows, 0))
        full = lax.dynamic_update_slice(full, mate, ((source ^ 1) * rows, 0))
        if step + 1 < count // 2:
            moving = lax.ppermute(moving, "dp", ring_perm(count))
            if step > 0:
                moving, _ = tie(moving, all_done)
    return full


def tie(*values):
    return lax.optimization_barrier(values)


def add(left, right):
    return left.astype(f32) + right.astype(f32)


def pick(values, at, axis):
    return lax.dynamic_index_in_dim(values, at, axis, keepdims=False)


def put(values, piece, at, axis):
    return lax.dynamic_update_index_in_dim(values, piece, at, axis)


def shift_perm(count, step):
    return [(i, (i + 2 * step) % count) for i in range(count)]


def gather_attention(shard):
    count = lax.axis_size("dp")
    if count > RING_MOST:
        return lax.all_gather(shard, ("dp", "expert"), axis=0, tiled=True), (shard,) * 3
    rows, cols = shard.shape
    outer = count // 2
    me = lax.axis_index("dp")
    line = me // 2
    quad = put(jnp.zeros((outer, rows, cols), shard.dtype), shard, line, 0)
    for step in range(1, outer):
        got = lax.ppermute(shard, "dp", shift_perm(count, step))
        quad = put(quad, got, lax.rem(line - step + outer, outer), 0)
    mate = lax.ppermute(quad, "dp", pair_perm(count))
    both = jnp.zeros((outer, 2, rows, cols), shard.dtype)
    both = put(put(both, quad, lax.rem(me, 2), 1), mate, 1 - lax.rem(me, 2), 1)
    across = swap(both, 2)
    full, corner = join_sides(both, across)
    return full, (got, mate, corner)


def join_sides(both, across):
    outer, _, rows, cols = both.shape
    sides, side = lax.axis_size("expert"), lax.axis_index("expert")
    full = jnp.zeros((outer, 2, sides, rows, cols), both.dtype)
    corner = swap(across, 1)
    full = put(full, both, side, 2)
    full = put(full, swap(both, 1), side ^ 1, 2)
    full = put(full, across, side ^ 2, 2)
    full = put(full, corner, side ^ 3, 2)
    return full.reshape(-1, cols), corner


def swap_pair(values):
    return lax.ppermute(values, "dp", pair_perm(lax.axis_size("dp")))


def ring_step(values):
    return lax.ppermute(values, "dp", ring_perm(lax.axis_size("dp")))


def ring_total(blocks):
    moving = blocks(lax.axis_size("dp") // 2 - 1)
    for step in reversed(range(lax.axis_size("dp") // 2 - 1)):
        moving = add(ring_step(moving), blocks(step))
        if step:
            moving = moving.astype(bf16)
    return moving


def halve_core(blocks, axis):
    core = lax.rem(lax.axis_index("expert"), 2)
    got = swap(pick(blocks, 1 - core, axis), 1)
    return add(pick(blocks, core, axis), got).astype(bf16)


def halve_line(blocks, axis):
    line = lax.axis_index("expert") // 2
    got = swap(pick(blocks, 1 - line, axis), 2)
    return add(pick(blocks, line, axis), got).astype(bf16)


def halve_pair(blocks, axis):
    mine = lax.rem(lax.axis_index("dp"), 2)
    got = lax.ppermute(pick(blocks, 1 - mine, axis), "dp", pair_perm(lax.axis_size("dp")))
    return add(pick(blocks, mine, axis), got).astype(bf16)


def reduce_line(blocks):
    count = lax.axis_size("dp")
    outer = count // 2
    line = lax.axis_index("dp") // 2
    total = pick(blocks, line, 0).astype(f32)
    for step in range(1, outer):
        sent = pick(blocks, lax.rem(line + step, outer), 0)
        total = total + lax.ppermute(sent, "dp", shift_perm(count, step)).astype(f32)
    return total


def attention_blocks(values):
    return values.reshape(lax.axis_size("dp") // 2, 2, lax.axis_size("expert") // 2, 2, -1, values.shape[1])


def reduce_everywhere(values):
    return lax.psum_scatter(values, ("dp", "expert"), scatter_dimension=0, tiled=True).astype(f32)


def on_device(
    tokens,
    groups,
    key_mask,
    routes,
    query_weight,
    key_weight,
    value_weight,
    output_weight,
    norm_first,
    norm_second,
    expert_in,
    expert_out,
    cotangent,
):
    both = ("dp", "expert")
    row_count, width = tokens.shape
    units = expert_in.shape[3]
    shard_rows = expert_in.shape[2]
    own_rows = query_weight.shape[1]

    attention_shards = whole_call(
        pack_body,
        [jax.ShapeDtypeStruct((own_rows, 4 * width + PAIR), bf16)] * LAYERS,
        name="pack_attention",
    )(query_weight, key_weight, value_weight, output_weight, norm_first, norm_second)

    def expert_shard(layer):
        pieces = jnp.concatenate(
            [expert_in[layer], jnp.transpose(expert_out[layer], (0, 2, 1))], 2
        )
        return jnp.transpose(pieces, (1, 0, 2)).reshape(shard_rows, EXPERTS * 2 * units)

    count = lax.axis_size("dp")
    small = count <= RING_MOST
    attention_first, events = gather_attention(attention_shards[0])
    attention_all = [
        attention_first,
        lax.all_gather(attention_shards[1], both, axis=0, tiled=True),
    ]
    experts_all = [
        gather_rows(expert_shard(0), events),
        lax.all_gather(expert_shard(1), "dp", axis=0, tiled=True),
    ]

    route = routes[:, 0]
    place = jnp.arange(row_count, dtype=jnp.int32)
    earlier = (route[:, None] == route[None, :]) & (place[None, :] < place[:, None])
    slot_of = route * MOST + jnp.sum(earlier.astype(jnp.int32), 1)
    spot = (slot_of[:, None] == jnp.arange(SLOTS, dtype=jnp.int32)[None, :]).astype(bf16)
    group = groups[0]
    allowed = (group[:, None] == group[None, :]) & (
        (key_mask[None, :] == 1) | (place[:, None] == place[None, :])
    )
    bias = jnp.where(allowed, 0.0, FAR).astype(f32)

    last_slots = contract_rows(spot, cotangent.astype(bf16)).astype(bf16)
    last_slots, _ = tie(last_slots, events[2])
    last_grads = spread_slots(last_slots)

    def shape_of(rows, cols, kind):
        return jax.ShapeDtypeStruct((rows, cols), kind)

    saved = []
    rows = tokens
    parts = None
    for layer in range(LAYERS):
        first = layer == 0
        weight = attention_all[layer]
        outs = whole_call(
            partial(attend_forward_body, first),
            [
                shape_of(row_count, 3 * width, bf16),
                shape_of(row_count, PAIR, f32),
                shape_of(row_count, width, bf16),
                shape_of(row_count, width, f32),
                shape_of(SLOTS, width, bf16),
            ]
            + ([] if first else [shape_of(row_count, width, f32)]),
            name="attend_forward",
        )(*([rows] if first else [rows, *parts]), spot, bias, weight)
        triple, logs, context, hidden, slots = outs[:5]
        inputs = tokens if first else outs[5]
        if first:
            slots, _ = tie(slots, last_grads[2])
        blocks = spread_slots(slots)
        sums, active, slope = expert_forward(blocks, experts_all[layer])
        if layer + 1 < LAYERS:
            parts = collect_slots(sums)
        rows = hidden
        saved.append((inputs, triple, logs, context, hidden, blocks, active, slope, weight))
    final_near, final_far = collect_core(sums)

    def expert_part(layer, grads, split):
        blocks, active, slope = saved[layer][5:8]
        return expert_backward(grads, blocks, active, slope, experts_all[layer], split)

    def attend_part(layer, parts, grad):
        inputs, triple, logs, context, hidden = saved[layer][:5]
        weight = saved[layer][8]
        last = layer == 0
        return whole_call(
            partial(attend_backward_body, last),
            [shape_of(row_count, width, f32), shape_of(width, 4 * width + PAIR, bf16)]
            + ([] if last else [shape_of(SLOTS, width, bf16)]),
            scratch_shapes=[
                pltpu.VMEM((row_count, width), bf16),
                pltpu.VMEM((row_count, 3 * width), bf16),
            ],
            name="attend_backward",
        )(*parts, grad, hidden, inputs, triple, logs, context, spot, bias, weight)

    def offload(values):
        return lax.psum_scatter(values, "dp", scatter_dimension=0, tiled=True)

    together = tuple((0, 2 * units * expert) for expert in range(EXPERTS))
    if small:
        sums, (whole,) = expert_part(1, last_grads, False)
        second_experts = offload(whole)
        parts = collect_slots(sums)
        *parts, final_near, final_far = tie(*parts, final_near, final_far)
        outs = attend_part(1, parts, cotangent)
        held = halve_core(attention_blocks(outs[1]), 3)
        grad_blocks = spread_slots(outs[2])
        *grad_blocks, held = tie(*grad_blocks, held)
        held = halve_line(held, 2)
        sums, pairs = expert_part(0, grad_blocks, True)
        held = halve_pair(held, 1)
        kepts = list(pairs[::2])
        gots = [swap_pair(sent) for sent in pairs[1::2]]
        parts = collect_slots(sums)
        outs = attend_part(0, parts, outs[0])
        whole, gots[0], second_experts = tie(outs[1], gots[0], second_experts)
        second_total = reduce_line(held)

        def block(expert, step):
            return add(kepts[expert][step], gots[expert][step]).astype(bf16)

        def onward(expert, moving, step):
            return add(moving, block(expert, step)).astype(bf16)

        blocks = halve_core(attention_blocks(whole), 3)
        blocks, kepts[0] = tie(blocks, kepts[0])
        blocks = halve_line(blocks, 2)
        one = ring_step(block(0, 3))
        one, kepts[1] = tie(one, kepts[1])
        one = ring_step(onward(0, one, 2))
        two = ring_step(block(1, 3))
        two, kepts[2], final_far = tie(two, kepts[2], final_far)
        final_far = swap(final_far, 2)
        first_total = reduce_line(halve_pair(blocks, 1))
        one = add(ring_step(onward(0, one, 1)), block(0, 0))
        two = ring_step(onward(1, two, 2))
        two = add(ring_step(onward(1, two, 1)), block(1, 0))
        three = ring_step(block(2, 3))
        three = ring_step(onward(2, three, 2))
        three = add(ring_step(onward(2, three, 1)), block(2, 0))
        first_experts = [one, two, three]
        places = (tuple((expert, 0) for expert in range(EXPERTS)), together)
    else:
        sums, (whole,) = expert_part(1, last_grads, False)
        second_experts = offload(whole)
        outs = attend_part(1, collect_slots(sums), cotangent)
        second_total = reduce_everywhere(outs[1])
        sums, (whole,) = expert_part(0, spread_slots(outs[2]), False)
        first_experts = [offload(whole)]
        outs = attend_part(0, collect_slots(sums), outs[0])
        first_total = reduce_everywhere(outs[1])
        final_far = swap(final_far, 2)
        places = (together, together)
    mixed = (rows + mat(spot, final_near) + mat(spot, final_far)).astype(bf16)
    square = jax.ShapeDtypeStruct((LAYERS, own_rows, width), f32)
    line = jax.ShapeDtypeStruct((LAYERS, own_rows), f32)
    wide = jax.ShapeDtypeStruct((LAYERS, EXPERTS, shard_rows, units), f32)
    deltas = whole_call(
        partial(finish_body, places), [square] * 4 + [line] * 2 + [wide] * 2, name="finish"
    )(*first_experts, first_total, second_experts, second_total)
    return (mixed, outs[0], *deltas[:7], jnp.swapaxes(deltas[7], 2, 3))


def solution(mesh):
    placed = (
        P(("dp", "expert"), None),
        P(("dp", "expert"), None),
        P(("dp", "expert")),
        P(("dp", "expert"), None),
        P(None, ("dp", "expert"), None),
        P(None, ("dp", "expert"), None),
        P(None, ("dp", "expert"), None),
        P(None, ("dp", "expert"), None),
        P(None, ("dp", "expert")),
        P(None, ("dp", "expert")),
        P(None, None, "dp", "expert"),
        P(None, None, "expert", "dp"),
        P(("dp", "expert"), None),
    )
    return jax.shard_map(
        on_device,
        mesh=mesh,
        in_specs=placed,
        out_specs=(
            P(("dp", "expert"), None),
            P(("dp", "expert"), None),
            P(None, ("dp", "expert"), None),
            P(None, ("dp", "expert"), None),
            P(None, ("dp", "expert"), None),
            P(None, ("dp", "expert"), None),
            P(None, ("dp", "expert")),
            P(None, ("dp", "expert")),
            P(None, None, "dp", "expert"),
            P(None, None, "expert", "dp"),
        ),
        check_vma=False,
    )
```

```python
from functools import partial

import jax
import jax.numpy as jnp
from jax import lax
from jax.experimental import pallas as pl
from jax.experimental.pallas import tpu as pltpu
from jax.sharding import PartitionSpec as P

HEADS = 12
HEAD_DIM = 64
EXPERTS = 3
LAYERS = 2
MOST = 144

SLOTS = EXPERTS * MOST
PAIR = 2 * HEAD_DIM
epsilon = 1e-05
score_scale = 0.125
FAR = -1e30
RING_MOST = 8
VMEM_BYTES = 56 << 20
f32 = jnp.float32
bf16 = jnp.bfloat16


def mat(left, right):
    return jnp.dot(left, right, preferred_element_type=f32)


def contract_rows(left, right):
    return lax.dot_general(left, right, (((0,), (0,)), ((), ())), preferred_element_type=f32)


def contract_cols(left, right):
    return lax.dot_general(left, right, (((1,), (1,)), ((), ())), preferred_element_type=f32)


def norm_parts(values):
    average = jnp.mean(values, -1, keepdims=True)
    centered = values - average
    spread = jnp.mean(centered * centered, -1, keepdims=True)
    rate = lax.rsqrt(spread + epsilon)
    return centered * rate, rate


def norm_back(unit, rate, scaled_grad):
    first = jnp.mean(scaled_grad, -1, keepdims=True)
    second = jnp.mean(scaled_grad * unit, -1, keepdims=True)
    return rate * (scaled_grad - first - unit * second)


def cost(micros):
    return pl.CostEstimate(
        flops=micros * 10**7, transcendentals=0, bytes_accessed=micros * 10**4
    )


def whole_call(body, out_shape, scratch_shapes=(), name=None, micros=15):
    return pl.pallas_call(
        body,
        out_shape=out_shape,
        scratch_shapes=scratch_shapes,
        compiler_params=pltpu.CompilerParams(vmem_limit_bytes=VMEM_BYTES),
        cost_estimate=cost(micros),
        name=name,
    )


def pack_body(*refs):
    weight_refs, gain_refs, out_refs = refs[:4], refs[4:6], refs[6:]
    rows, width = weight_refs[0].shape[1:]
    lane = lax.broadcasted_iota(jnp.int32, (rows, PAIR), 1)
    diagonal = lax.broadcasted_iota(jnp.int32, (rows, rows), 0) == lax.broadcasted_iota(
        jnp.int32, (rows, rows), 1
    )
    for layer, out_ref in enumerate(out_refs):
        for place, weight_ref in enumerate(weight_refs):
            out_ref[:, place * width : (place + 1) * width] = weight_ref[layer]
        columns = [
            jnp.sum(jnp.where(diagonal, ref[layer : layer + 1, :].astype(f32), 0.0), 1, keepdims=True)
            for ref in gain_refs
        ]
        out_ref[:, 4 * width :] = jnp.where(
            lane == 0, columns[0], jnp.where(lane == 1, columns[1], 0.0)
        ).astype(bf16)


def attend_forward_body(first, *refs):
    if first:
        rows_ref, spot_ref, bias_ref, weight_ref = refs[:4]
        outs = refs[4:]
        rows = rows_ref[...].astype(f32)
    else:
        rows_ref, part_a_ref, part_b_ref, spot_ref, bias_ref, weight_ref = refs[:6]
        outs = refs[6:]
        spot = spot_ref[...]
        rows = rows_ref[...] + mat(spot, part_a_ref[...]) + mat(spot, part_b_ref[...])
    width = rows.shape[1]
    gains = weight_ref[:, 4 * width :].astype(f32).T
    triple_ref, logs_ref, context_ref, hidden_ref, slots_ref = outs[:5]
    if not first:
        outs[5][...] = rows
    unit, _ = norm_parts(rows)
    normed = (unit * gains[0:1, :]).astype(bf16)
    triple_ref[...] = mat(normed, weight_ref[:, : 3 * width]).astype(bf16)
    row_count = rows.shape[0]
    lane = lax.broadcasted_iota(jnp.int32, (row_count, PAIR), 1)
    logs_ref[...] = jnp.zeros_like(logs_ref)

    def one_pair(pair, carry):
        at = pl.multiple_of(pair * PAIR, PAIR)
        query = triple_ref[:, pl.ds(at, PAIR)]
        key = triple_ref[:, pl.ds(at + width, PAIR)]
        value = triple_ref[:, pl.ds(at + 2 * width, PAIR)]
        sides = []
        logs = logs_ref[...]
        for side in range(2):
            mine = (lane >= HEAD_DIM) if side else (lane < HEAD_DIM)
            scores = contract_cols(jnp.where(mine, query, jnp.zeros((), bf16)), key)
            scores = scores * score_scale + bias_ref[...]
            highest = jnp.max(scores, 1, keepdims=True)
            powers = jnp.exp(scores - highest)
            totals = jnp.sum(powers, 1, keepdims=True)
            probs = (powers * (1.0 / totals)).astype(bf16)
            sides.append(mat(probs, value))
            logs = jnp.where(lane == 2 * pair + side, highest + jnp.log(totals), logs)
        logs_ref[...] = logs
        context_ref[:, pl.ds(at, PAIR)] = jnp.where(lane < HEAD_DIM, sides[0], sides[1]).astype(bf16)
        return carry

    lax.fori_loop(0, HEADS // 2, one_pair, 0)
    hidden = rows + mat(context_ref[...], weight_ref[:, 3 * width : 4 * width])
    hidden_ref[...] = hidden
    unit, _ = norm_parts(hidden)
    second = (unit * gains[1:2, :]).astype(bf16)
    slots_ref[...] = contract_rows(spot_ref[...], second).astype(bf16)


def attend_backward_body(last, *refs):
    (
        part_a_ref,
        part_b_ref,
        grad_ref,
        hidden_ref,
        rows_ref,
        triple_ref,
        logs_ref,
        context_ref,
        spot_ref,
        bias_ref,
        weight_ref,
    ) = refs[:11]
    slots_ref = None
    grad_out_ref, weight_grad_ref = refs[11:13]
    if not last:
        slots_ref = refs[13]
    context_grad_ref, triple_grad_ref = refs[-2:]
    width = rows_ref.shape[1]
    gains = weight_ref[:, 4 * width :].astype(f32).T
    spot = spot_ref[...]
    second_grad = mat(spot, part_a_ref[...]) + mat(spot, part_b_ref[...])
    unit, rate = norm_parts(hidden_ref[...])
    second_gain_grad = jnp.sum(second_grad * unit, 0, keepdims=True)
    hidden_grad = grad_ref[...] + norm_back(unit, rate, second_grad * gains[1:2, :])
    row_count, width = hidden_grad.shape
    grad_out_ref[...] = hidden_grad
    branch = hidden_grad.astype(bf16)
    context_grad_ref[...] = contract_cols(branch, weight_ref[:, 3 * width : 4 * width]).astype(bf16)
    output_grad = contract_rows(context_ref[...], branch).astype(bf16)
    weight_grad_ref[:, 3 * width : 4 * width] = output_grad
    lane = lax.broadcasted_iota(jnp.int32, (row_count, PAIR), 1)

    def one_pair(pair, carry):
        at = pl.multiple_of(pair * PAIR, PAIR)
        query = triple_ref[:, pl.ds(at, PAIR)]
        key = triple_ref[:, pl.ds(at + width, PAIR)]
        value = triple_ref[:, pl.ds(at + 2 * width, PAIR)]
        gone = context_grad_ref[:, pl.ds(at, PAIR)]
        zero = jnp.zeros((), bf16)
        query_sides, key_sides, value_sides = [], [], []
        for side in range(2):
            mine = (lane >= HEAD_DIM) if side else (lane < HEAD_DIM)
            log_total = jnp.sum(
                jnp.where(lane == 2 * pair + side, logs_ref[...], 0.0), 1, keepdims=True
            )
            scores = contract_cols(jnp.where(mine, query, zero), key)
            scores = scores * score_scale + bias_ref[...]
            probs = jnp.exp(scores - log_total)
            prob_grad = contract_cols(jnp.where(mine, gone, zero), value)
            inner = jnp.sum(probs * prob_grad, 1, keepdims=True)
            score_grad = (probs * (prob_grad - inner)).astype(bf16)
            query_sides.append(mat(score_grad, key))
            key_sides.append(contract_rows(score_grad, query))
            value_sides.append(contract_rows(probs.astype(bf16), gone))
        left = lane < HEAD_DIM
        triple_grad_ref[:, pl.ds(at, PAIR)] = (
            score_scale * jnp.where(left, query_sides[0], query_sides[1])
        ).astype(bf16)
        triple_grad_ref[:, pl.ds(at + width, PAIR)] = (
            score_scale * jnp.where(left, key_sides[0], key_sides[1])
        ).astype(bf16)
        triple_grad_ref[:, pl.ds(at + 2 * width, PAIR)] = jnp.where(
            left, value_sides[0], value_sides[1]
        ).astype(bf16)
        return carry

    lax.fori_loop(0, HEADS // 2, one_pair, 0)
    unit, rate = norm_parts(rows_ref[...].astype(f32))
    normed = (unit * gains[0:1, :]).astype(bf16)
    triple_grad = triple_grad_ref[...]
    weight_grad_ref[:, : 3 * width] = contract_rows(normed, triple_grad).astype(bf16)
    normed_grad = contract_cols(triple_grad, weight_ref[:, : 3 * width])
    first_gain_grad = jnp.sum(normed_grad * unit, 0, keepdims=True)
    out_grad = grad_out_ref[...] + norm_back(unit, rate, normed_grad * gains[0:1, :])
    grad_out_ref[...] = out_grad
    if slots_ref is not None:
        slots_ref[...] = contract_rows(spot, out_grad.astype(bf16)).astype(bf16)
    which = lax.broadcasted_iota(jnp.int32, (PAIR, width), 0)
    gain_rows = jnp.where(
        which == 0, first_gain_grad, jnp.where(which == 1, second_gain_grad, 0.0)
    )
    weight_grad_ref[:, 4 * width :] = gain_rows.T.astype(bf16)


def expert_forward_body(*refs):
    block_refs, weight_ref = refs[:4], refs[4]
    out_refs, active_ref, slope_ref = refs[5:9], refs[9], refs[10]
    width = block_refs[0].shape[1]
    units = weight_ref.shape[1] // 2
    for half in range(2):
        rows = jnp.concatenate([block_refs[2 * half][...], block_refs[2 * half + 1][...]], 0)
        before = mat(rows, weight_ref[:, :units])
        share = 0.5 + 0.5 * lax.erf(before * 0.7071067811865476)
        slope = share + before * (0.3989422804014327 * jnp.exp(-0.5 * before * before))
        active = (before * share).astype(bf16)
        span = slice(half * 2 * MOST, (half + 1) * 2 * MOST)
        active_ref[span, :] = active
        slope_ref[span, :] = slope.astype(bf16)
        sums = contract_cols(active, weight_ref[:, units:]).astype(bf16)
        out_refs[2 * half][...] = sums[:MOST]
        out_refs[2 * half + 1][...] = sums[MOST:]


def expert_backward_body(split, *refs):
    place_ref, *refs = refs
    grad_refs, block_refs = refs[:4], refs[4:8]
    active_ref, slope_ref, weight_ref = refs[8:11]
    out_refs, total_refs = refs[11:15], refs[15:]
    units = weight_ref.shape[1] // 2
    grads = jnp.concatenate([ref[...] for ref in grad_refs], 0)
    rows = jnp.concatenate([ref[...] for ref in block_refs], 0)
    active_grad = mat(grads, weight_ref[:, units:])
    before_grad = (active_grad * slope_ref[...].astype(f32)).astype(bf16)
    sums = contract_cols(before_grad, weight_ref[:, :units]).astype(bf16)
    for place in range(4):
        out_refs[place][...] = sums[place * MOST : (place + 1) * MOST]
    step = pl.program_id(0)
    for left, right, start in ((rows, before_grad, 0), (grads, active_ref[...], units)):
        grad = contract_rows(left, right).astype(bf16)
        span = slice(start, start + units)
        if not split:
            total_refs[0][:, span] = grad
            continue
        ring, mine = place_ref[0], place_ref[1]
        outer, count = total_refs[0].shape[:2]

        def piece(block, half):
            first = (2 * block + half) * count
            return grad[first : first + count]

        for expert in range(EXPERTS):
            for half in range(2):

                @pl.when((step == expert) & (mine == half))
                def _():
                    for block in range(outer):
                        at = lax.rem(block - ring + outer, outer)
                        kept_ref, sent_ref = total_refs[2 * expert : 2 * expert + 2]
                        kept_ref[at, :, span] = piece(block, half)
                        sent_ref[at, :, span] = piece(block, 1 - half)


def finish_body(places, *refs):
    outs = refs[-8:]
    at = 0
    units = outs[6].shape[3]
    for layer, experts in enumerate(places):
        for expert, (source, start) in enumerate(experts):
            values = refs[at + source]
            outs[6][layer, expert] = values[:, start : start + units].astype(f32)
            outs[7][layer, expert] = values[:, start + units : start + 2 * units].astype(f32)
        at += max(source for source, _ in experts) + 1
        sums = refs[at][...].astype(f32)
        at += 1
        rows, width = outs[0].shape[1:]
        for place in range(4):
            outs[place][layer] = sums[:, place * width : (place + 1) * width]
        diagonal = lax.broadcasted_iota(jnp.int32, (rows, rows), 0) == lax.broadcasted_iota(
            jnp.int32, (rows, rows), 1
        )
        for place in range(2):
            column = sums[:, 4 * width + place : 4 * width + place + 1]
            outs[4 + place][layer : layer + 1, :] = jnp.sum(
                jnp.where(diagonal, column, 0.0), 0, keepdims=True
            )


def expert_forward(blocks, weights):
    width = blocks[0].shape[1]
    units = weights.shape[1] // (2 * EXPERTS)
    block = pl.BlockSpec((MOST, width), lambda e: (e, 0))
    kept = pl.BlockSpec((4 * MOST, units), lambda e: (e, 0))
    outs = pl.pallas_call(
        expert_forward_body,
        grid=(EXPERTS,),
        in_specs=[block] * 4 + [pl.BlockSpec((width, 2 * units), lambda e: (0, e))],
        out_specs=[block] * 4 + [kept] * 2,
        out_shape=[jax.ShapeDtypeStruct((SLOTS, width), bf16)] * 4
        + [jax.ShapeDtypeStruct((4 * SLOTS, units), bf16)] * 2,
        compiler_params=pltpu.CompilerParams(vmem_limit_bytes=VMEM_BYTES),
        cost_estimate=cost(10),
        name="expert_forward",
    )(*blocks, weights)
    return outs[:4], outs[4], outs[5]


def expert_backward(grads, blocks, active, slope, weights, split):
    width = blocks[0].shape[1]
    units = weights.shape[1] // (2 * EXPERTS)
    count, me = lax.axis_size("dp"), lax.axis_index("dp")
    block = pl.BlockSpec((MOST, width), lambda e, *_: (e, 0))
    kept = pl.BlockSpec((4 * MOST, units), lambda e, *_: (e, 0))
    square = pl.BlockSpec((width, 2 * units), lambda e, *_: (0, e))
    out_specs = [block] * 4
    out_shape = [jax.ShapeDtypeStruct((SLOTS, width), bf16)] * 4
    if split:
        pair = (count // 2, width // count, 2 * units)
        out_specs += [pl.BlockSpec(pair, lambda e, *_: (0, 0, 0))] * (2 * EXPERTS)
        out_shape += [jax.ShapeDtypeStruct(pair, bf16)] * (2 * EXPERTS)
    else:
        out_specs += [square]
        out_shape += [jax.ShapeDtypeStruct(weights.shape, bf16)]
    outs = pl.pallas_call(
        partial(expert_backward_body, split),
        grid_spec=pltpu.PrefetchScalarGridSpec(
            num_scalar_prefetch=1,
            grid=(EXPERTS,),
            in_specs=[block] * 8 + [kept] * 2 + [square],
            out_specs=out_specs,
        ),
        out_shape=out_shape,
        compiler_params=pltpu.CompilerParams(vmem_limit_bytes=VMEM_BYTES),
        cost_estimate=cost(16),
        name="expert_backward",
    )(
        jnp.stack([me // 2, lax.rem(me, 2)]).astype(jnp.int32),
        *grads,
        *blocks,
        active,
        slope,
        weights,
    )
    return outs[:4], outs[4:]


def swap(values, flip):
    count = lax.axis_size("expert")
    return lax.ppermute(values, "expert", [(i, i ^ flip) for i in range(count)])


def spread_slots(slots):
    across = swap(slots, 2)
    beside = swap(slots, 1)
    corner = swap(across, 1)
    return [slots, beside, across, corner]


def collect_core(parts):
    own, beside, across, corner = parts
    corner_in = swap(corner, 1)
    beside_in = swap(beside, 1)
    far = (across.astype(f32) + corner_in.astype(f32)).astype(bf16)
    near = (own.astype(f32) + beside_in.astype(f32)).astype(bf16)
    return near, far


def collect_slots(parts):
    near, far = collect_core(parts)
    return near, swap(far, 2)


def pair_perm(count):
    return [(i, i ^ 1) for i in range(count)]


def ring_perm(count):
    return [(i, (i + 2) % count) for i in range(count)]


def gather_rows(shard, events):
    count = lax.axis_size("dp")
    if count > RING_MOST:
        return lax.all_gather(shard, "dp", axis=0, tiled=True)
    line_done, pair_done, all_done = events
    me = lax.axis_index("dp")
    rows, cols = shard.shape
    full = jnp.zeros((count * rows, cols), shard.dtype)
    moving, _ = tie(shard, line_done)
    for step in range(count // 2):
        source = lax.rem(me - 2 * step + count, count)
        mate = moving
        if step == 0:
            mate, _ = tie(mate, pair_done)
        mate = lax.ppermute(mate, "dp", pair_perm(count))
        mate, _ = tie(mate, all_done)
        full = lax.dynamic_update_slice(full, moving, (source * rows, 0))
        full = lax.dynamic_update_slice(full, mate, ((source ^ 1) * rows, 0))
        if step + 1 < count // 2:
            moving = lax.ppermute(moving, "dp", ring_perm(count))
            if step > 0:
                moving, _ = tie(moving, all_done)
    return full


def tie(*values):
    return lax.optimization_barrier(values)


def add(left, right):
    return left.astype(f32) + right.astype(f32)


def pick(values, at, axis):
    return lax.dynamic_index_in_dim(values, at, axis, keepdims=False)


def put(values, piece, at, axis):
    return lax.dynamic_update_index_in_dim(values, piece, at, axis)


def shift_perm(count, step):
    return [(i, (i + 2 * step) % count) for i in range(count)]


def gather_attention(shard):
    count = lax.axis_size("dp")
    if count > RING_MOST:
        return lax.all_gather(shard, ("dp", "expert"), axis=0, tiled=True), (shard,) * 3
    rows, cols = shard.shape
    outer = count // 2
    me = lax.axis_index("dp")
    line = me // 2
    quad = put(jnp.zeros((outer, rows, cols), shard.dtype), shard, line, 0)
    for step in range(1, outer):
        got = lax.ppermute(shard, "dp", shift_perm(count, step))
        quad = put(quad, got, lax.rem(line - step + outer, outer), 0)
    mate = lax.ppermute(quad, "dp", pair_perm(count))
    both = jnp.zeros((outer, 2, rows, cols), shard.dtype)
    both = put(put(both, quad, lax.rem(me, 2), 1), mate, 1 - lax.rem(me, 2), 1)
    across = swap(both, 2)
    full, corner = join_sides(both, across)
    return full, (got, mate, corner)


def join_sides(both, across):
    outer, _, rows, cols = both.shape
    sides, side = lax.axis_size("expert"), lax.axis_index("expert")
    full = jnp.zeros((outer, 2, sides, rows, cols), both.dtype)
    corner = swap(across, 1)
    full = put(full, both, side, 2)
    full = put(full, swap(both, 1), side ^ 1, 2)
    full = put(full, across, side ^ 2, 2)
    full = put(full, corner, side ^ 3, 2)
    return full.reshape(-1, cols), corner


def swap_pair(values):
    return lax.ppermute(values, "dp", pair_perm(lax.axis_size("dp")))


def ring_step(values):
    return lax.ppermute(values, "dp", ring_perm(lax.axis_size("dp")))


def ring_total(blocks):
    moving = blocks(lax.axis_size("dp") // 2 - 1)
    for step in reversed(range(lax.axis_size("dp") // 2 - 1)):
        moving = add(ring_step(moving), blocks(step))
        if step:
            moving = moving.astype(bf16)
    return moving


def halve_core(blocks, axis):
    core = lax.rem(lax.axis_index("expert"), 2)
    got = swap(pick(blocks, 1 - core, axis), 1)
    return add(pick(blocks, core, axis), got).astype(bf16)


def halve_line(blocks, axis):
    line = lax.axis_index("expert") // 2
    got = swap(pick(blocks, 1 - line, axis), 2)
    return add(pick(blocks, line, axis), got).astype(bf16)


def halve_pair(blocks, axis):
    mine = lax.rem(lax.axis_index("dp"), 2)
    got = lax.ppermute(pick(blocks, 1 - mine, axis), "dp", pair_perm(lax.axis_size("dp")))
    return add(pick(blocks, mine, axis), got).astype(bf16)


def reduce_line(blocks):
    count = lax.axis_size("dp")
    outer = count // 2
    line = lax.axis_index("dp") // 2
    total = pick(blocks, line, 0).astype(f32)
    for step in range(1, outer):
        sent = pick(blocks, lax.rem(line + step, outer), 0)
        total = total + lax.ppermute(sent, "dp", shift_perm(count, step)).astype(f32)
    return total


def attention_blocks(values):
    return values.reshape(lax.axis_size("dp") // 2, 2, lax.axis_size("expert") // 2, 2, -1, values.shape[1])


def reduce_everywhere(values):
    return lax.psum_scatter(values, ("dp", "expert"), scatter_dimension=0, tiled=True).astype(f32)


def on_device(
    tokens,
    groups,
    key_mask,
    routes,
    query_weight,
    key_weight,
    value_weight,
    output_weight,
    norm_first,
    norm_second,
    expert_in,
    expert_out,
    cotangent,
):
    both = ("dp", "expert")
    row_count, width = tokens.shape
    units = expert_in.shape[3]
    shard_rows = expert_in.shape[2]
    own_rows = query_weight.shape[1]

    attention_shards = whole_call(
        pack_body,
        [jax.ShapeDtypeStruct((own_rows, 4 * width + PAIR), bf16)] * LAYERS,
        name="pack_attention",
    )(query_weight, key_weight, value_weight, output_weight, norm_first, norm_second)

    def expert_shard(layer):
        pieces = jnp.concatenate(
            [expert_in[layer], jnp.transpose(expert_out[layer], (0, 2, 1))], 2
        )
        return jnp.transpose(pieces, (1, 0, 2)).reshape(shard_rows, EXPERTS * 2 * units)

    count = lax.axis_size("dp")
    small = count <= RING_MOST
    attention_first, events = gather_attention(attention_shards[0])
    attention_all = [
        attention_first,
        lax.all_gather(attention_shards[1], both, axis=0, tiled=True),
    ]
    experts_all = [
        gather_rows(expert_shard(0), events),
        lax.all_gather(expert_shard(1), "dp", axis=0, tiled=True),
    ]

    route = routes[:, 0]
    place = jnp.arange(row_count, dtype=jnp.int32)
    earlier = (route[:, None] == route[None, :]) & (place[None, :] < place[:, None])
    slot_of = route * MOST + jnp.sum(earlier.astype(jnp.int32), 1)
    spot = (slot_of[:, None] == jnp.arange(SLOTS, dtype=jnp.int32)[None, :]).astype(bf16)
    group = groups[0]
    allowed = (group[:, None] == group[None, :]) & (
        (key_mask[None, :] == 1) | (place[:, None] == place[None, :])
    )
    bias = jnp.where(allowed, 0.0, FAR).astype(f32)

    last_slots = contract_rows(spot, cotangent.astype(bf16)).astype(bf16)
    last_slots, _ = tie(last_slots, events[2])
    last_grads = spread_slots(last_slots)

    def shape_of(rows, cols, kind):
        return jax.ShapeDtypeStruct((rows, cols), kind)

    saved = []
    rows = tokens
    parts = None
    for layer in range(LAYERS):
        first = layer == 0
        weight = attention_all[layer]
        outs = whole_call(
            partial(attend_forward_body, first),
            [
                shape_of(row_count, 3 * width, bf16),
                shape_of(row_count, PAIR, f32),
                shape_of(row_count, width, bf16),
                shape_of(row_count, width, f32),
                shape_of(SLOTS, width, bf16),
            ]
            + ([] if first else [shape_of(row_count, width, f32)]),
            name="attend_forward",
        )(*([rows] if first else [rows, *parts]), spot, bias, weight)
        triple, logs, context, hidden, slots = outs[:5]
        inputs = tokens if first else outs[5]
        if first:
            slots, _ = tie(slots, last_grads[2])
        blocks = spread_slots(slots)
        sums, active, slope = expert_forward(blocks, experts_all[layer])
        if layer + 1 < LAYERS:
            parts = collect_slots(sums)
        rows = hidden
        saved.append((inputs, triple, logs, context, hidden, blocks, active, slope, weight))
    final_near, final_far = collect_core(sums)

    def expert_part(layer, grads, split):
        blocks, active, slope = saved[layer][5:8]
        return expert_backward(grads, blocks, active, slope, experts_all[layer], split)

    def attend_part(layer, parts, grad):
        inputs, triple, logs, context, hidden = saved[layer][:5]
        weight = saved[layer][8]
        last = layer == 0
        return whole_call(
            partial(attend_backward_body, last),
            [shape_of(row_count, width, f32), shape_of(width, 4 * width + PAIR, bf16)]
            + ([] if last else [shape_of(SLOTS, width, bf16)]),
            scratch_shapes=[
                pltpu.VMEM((row_count, width), bf16),
                pltpu.VMEM((row_count, 3 * width), bf16),
            ],
            name="attend_backward",
        )(*parts, grad, hidden, inputs, triple, logs, context, spot, bias, weight)

    def offload(values):
        return lax.psum_scatter(values, "dp", scatter_dimension=0, tiled=True)

    together = tuple((0, 2 * units * expert) for expert in range(EXPERTS))
    if small:
        sums, (whole,) = expert_part(1, last_grads, False)
        second_experts = offload(whole)
        parts = collect_slots(sums)
        *parts, final_near, final_far = tie(*parts, final_near, final_far)
        outs = attend_part(1, parts, cotangent)
        held = halve_core(attention_blocks(outs[1]), 3)
        grad_blocks = spread_slots(outs[2])
        *grad_blocks, held = tie(*grad_blocks, held)
        held = halve_line(held, 2)
        sums, pairs = expert_part(0, grad_blocks, True)
        held = halve_pair(held, 1)
        kepts = list(pairs[::2])
        gots = [swap_pair(sent) for sent in pairs[1::2]]
        parts = collect_slots(sums)
        outs = attend_part(0, parts, outs[0])
        whole, gots[0], second_experts = tie(outs[1], gots[0], second_experts)
        second_total = reduce_line(held)

        def block(expert, step):
            return add(kepts[expert][step], gots[expert][step]).astype(bf16)

        def onward(expert, moving, step):
            return add(moving, block(expert, step)).astype(bf16)

        blocks = halve_core(attention_blocks(whole), 3)
        blocks, kepts[0] = tie(blocks, kepts[0])
        blocks = halve_line(blocks, 2)
        one = ring_step(block(0, 3))
        one, kepts[1] = tie(one, kepts[1])
        one = ring_step(onward(0, one, 2))
        two = ring_step(block(1, 3))
        two, kepts[2], final_far = tie(two, kepts[2], final_far)
        final_far = swap(final_far, 2)
        first_total = reduce_line(halve_pair(blocks, 1))
        one = add(ring_step(onward(0, one, 1)), block(0, 0))
        two = ring_step(onward(1, two, 2))
        two = add(ring_step(onward(1, two, 1)), block(1, 0))
        three = ring_step(block(2, 3))
        three = ring_step(onward(2, three, 2))
        three = add(ring_step(onward(2, three, 1)), block(2, 0))
        first_experts = [one, two, three]
        places = (tuple((expert, 0) for expert in range(EXPERTS)), together)
    else:
        sums, (whole,) = expert_part(1, last_grads, False)
        second_experts = offload(whole)
        outs = attend_part(1, collect_slots(sums), cotangent)
        second_total = reduce_everywhere(outs[1])
        sums, (whole,) = expert_part(0, spread_slots(outs[2]), False)
        first_experts = [offload(whole)]
        outs = attend_part(0, collect_slots(sums), outs[0])
        first_total = reduce_everywhere(outs[1])
        final_far = swap(final_far, 2)
        places = (together, together)
    mixed = (rows + mat(spot, final_near) + mat(spot, final_far)).astype(bf16)
    square = jax.ShapeDtypeStruct((LAYERS, own_rows, width), f32)
    line = jax.ShapeDtypeStruct((LAYERS, own_rows), f32)
    wide = jax.ShapeDtypeStruct((LAYERS, EXPERTS, shard_rows, units), f32)
    deltas = whole_call(
        partial(finish_body, places), [square] * 4 + [line] * 2 + [wide] * 2, name="finish"
    )(*first_experts, first_total, second_experts, second_total)
    return (mixed, outs[0], *deltas[:7], jnp.swapaxes(deltas[7], 2, 3))


def solution(mesh):
    placed = (
        P(("dp", "expert"), None),
        P(("dp", "expert"), None),
        P(("dp", "expert")),
        P(("dp", "expert"), None),
        P(None, ("dp", "expert"), None),
        P(None, ("dp", "expert"), None),
        P(None, ("dp", "expert"), None),
        P(None, ("dp", "expert"), None),
        P(None, ("dp", "expert")),
        P(None, ("dp", "expert")),
        P(None, None, "dp", "expert"),
        P(None, None, "expert", "dp"),
        P(("dp", "expert"), None),
    )
    return jax.shard_map(
        on_device,
        mesh=mesh,
        in_specs=placed,
        out_specs=(
            P(("dp", "expert"), None),
            P(("dp", "expert"), None),
            P(None, ("dp", "expert"), None),
            P(None, ("dp", "expert"), None),
            P(None, ("dp", "expert"), None),
            P(None, ("dp", "expert"), None),
            P(None, ("dp", "expert")),
            P(None, ("dp", "expert")),
            P(None, None, "dp", "expert"),
            P(None, None, "expert", "dp"),
        ),
        check_vma=False,
    )
```
